1024 devices in a mesh: tile: 16 (over z_lo, y), date: 64 (over z_hi, x, core).
Axes of the slice: x: 8, y: 8, z: 8 (z_hi: 4, z_lo: 2; z = z_hi * 2 + z_lo), core: 2. Of those that a mesh axis runs over, the one named last changes fastest.
Arguments:
- layer_input: bfloat16 [1024, 256, 1024], P('tile', 'date'), may hold values from -6 to 6
- head_input: bfloat16 [1024, 256, 1024], P('tile', 'date'), may hold values from -6 to 6
- out_grad: bfloat16 [1024, 256, 1024], P('tile', 'date'), may hold values from -6 to 6
- sensor_ids: int32 [256], P('date'), may hold values from 0 to 1
- valid_mask: int32 [1024, 256], P('tile', 'date'), may hold values 0 or 1
- sensor_table: float32 [2, 1024], replicated, may hold values from -4 to 4
- proj_weight: bfloat16 [1024, 264], replicated, may hold values from -0.09375 to 0.09375
- step_bias: float32 [8], replicated, may hold values from -4 to -2
- decay_log: float32 [8], replicated, may hold values from -4 to 0
- skip_gain: float32 [8], replicated, may hold values from 0.5 to 1.5
Outputs:
- value_grad: bfloat16 [1024, 256, 1024], P('tile', 'date')
- input_grad: bfloat16 [1024, 256, 1024], P('tile', 'date')
- weight_grad: float32 [1024, 264], replicated
- table_grad: float32 [2, 1024], replicated
- head_grads: float32 [3, 8], replicated
The draws below stay inside these ranges and needn't reach their ends.
All inputs are finite; a program needn't handle non-finite values. No bound on the sum of `valid_mask` on one device may be relied on, other than what follows from the above.
Results may differ from the reference program's by a relative error of at most 0.0088.
Values may be sent and summed in bfloat16 or wider, within the bound.
A program may use at most 64 MiB of HBM per device.

```python
import math
import jax
import jax.numpy as jnp
from jax import lax

D = 1024
H = 8
P_SIZE = 128
N = 128
SPAN = 64
L = 256
PIX = 1024
N_TILE = 16


def set_ends(values, own_key, least, high):
    extent = values.shape
    index_at = [jax.random.randint(jax.random.fold_in(own_key, axis), (), 0, extent[axis]) for axis in range(len(extent))]
    values = values.at[tuple(index_at)].set(least)
    longest = extent.index(max(extent))
    index_at[longest] = (index_at[longest] + 1) % extent[longest]
    return values.at[tuple(index_at)].set(high)


def block_levels(rng, dims, split, low, high):
    def one(dim, shards_of):
        steps = jax.random.uniform(jax.random.fold_in(jax.random.fold_in(rng, 6), dim), (shards_of,), jnp.float32, low / len(split), high / len(split))
        return jnp.repeat(jnp.exp(steps), dims[dim] // shards_of).reshape((-1,) + (1,) * (len(dims) - dim - 1))

    factor_of = one(*split[0])
    for cut in split[1:]:
        factor_of = factor_of * one(*cut)
    return factor_of


def centred(own_key, dims, scale, limit, split=(), held_as=jnp.bfloat16):
    gain = block_levels(own_key, dims, split, -0.22, 0.18) if split else 1.0
    values = jax.random.normal(own_key, dims, jnp.float32) * scale * gain
    return jnp.minimum(jnp.maximum(values, -limit), limit).astype(held_as)


def setup_inputs(seed: int = 0) -> dict:
    key_list = jax.random.split(jax.random.key(seed), 11)
    layer_input = centred(key_list[0], (PIX, L, D), 1.0, 6.0, ((0, 16), (1, 64)))
    head_input = centred(key_list[1], (PIX, L, H * P_SIZE), 1.0, 6.0, ((0, 16), (1, 64)))
    out_grad = centred(key_list[2], (PIX, L, H * P_SIZE), 1.0, 6.0, ((0, 16), (1, 64)))
    sensor_ids = set_ends(jax.random.randint(key_list[3], (L,), 0, 2), jax.random.fold_in(key_list[3], 1), 0, 1).astype(jnp.int32)
    valid_mask = set_ends((jax.random.randint(key_list[4], (PIX, L), 0, 5) < 4).astype(jnp.int32), jax.random.fold_in(key_list[4], 1), 0, 1)
    sensor_table = centred(key_list[5], (2, D), 1.0, 4.0, (), jnp.float32)
    proj_weight = centred(key_list[6], (D, 2 * N + H), (4 * D) ** -0.5, 0.09375)
    step_bias = jnp.clip(jax.random.uniform(key_list[7], (H,), jnp.float32, -4.0, -2.0), -4.0, -2.0)
    decay_log = jnp.clip(jax.random.uniform(key_list[8], (H,), jnp.float32, -4.0, 0.0), -4.0, 0.0)
    skip_gain = jnp.clip(jax.random.uniform(key_list[9], (H,), jnp.float32, 0.5, 1.5), 0.5, 1.5)
    return dict(layer_input=layer_input, head_input=head_input, out_grad=out_grad, sensor_ids=sensor_ids, valid_mask=valid_mask, sensor_table=sensor_table, proj_weight=proj_weight, step_bias=step_bias, decay_log=decay_log, skip_gain=skip_gain)


HIGHEST_PREC = lax.Precision.HIGHEST
NEG_FILL = -1e+30

def span_scan(values_in, keys_in, reads_in, step_in, decay_in, skip_in, block_len):
    series, length, head_count, width_p = values_in.shape
    states_n = keys_in.shape[2]
    block_count = length // block_len
    decay_rate = -jnp.exp(decay_in)
    values_blk = values_in.reshape(series, block_count, block_len, head_count, width_p)
    keys_b = keys_in.reshape(series, block_count, block_len, states_n)
    reads_c = reads_in.reshape(series, block_count, block_len, states_n)
    step_blocks = step_in.reshape(series, block_count, block_len, head_count)
    weighted = values_blk * step_blocks[..., None]
    log_decay = jnp.cumsum(step_blocks * decay_rate, axis=2)
    log_heads = jnp.swapaxes(log_decay, 2, 3)
    row_ids = lax.broadcasted_iota(jnp.int32, (block_len, block_len), 0)
    col_ids = lax.broadcasted_iota(jnp.int32, (block_len, block_len), 1)
    causal = row_ids >= col_ids
    gap_logs = log_heads[..., :, None] - log_heads[..., None, :]
    kernel = jnp.exp(jnp.where(causal, gap_logs, NEG_FILL))
    scores = jnp.einsum('scin,scjn->scij', reads_c, keys_b, precision=HIGHEST_PREC)
    mixed_kernel = kernel * scores[:, :, None]
    within_block = jnp.einsum('schij,scjhp->scihp', mixed_kernel, weighted, precision=HIGHEST_PREC)
    to_block_end = jnp.exp(log_decay[:, :, -1:, :] - log_decay)
    block_states = jnp.einsum('scjn,scjhp->schnp', keys_b, weighted * to_block_end[..., None], precision=HIGHEST_PREC)
    block_totals = jnp.exp(log_decay[:, :, -1, :])

    def advance(state_carry, block_item):
        block_total, block_state = block_item
        return (state_carry * block_total[:, :, None, None] + block_state, state_carry)
    zero_state = jnp.zeros((series, head_count, states_n, width_p), dtype=values_in.dtype)
    _, entering = lax.scan(advance, zero_state, (jnp.moveaxis(block_totals, 1, 0), jnp.moveaxis(block_states, 1, 0)))
    entering = jnp.moveaxis(entering, 0, 1)
    from_earlier = jnp.einsum('scin,schnp->scihp', reads_c, entering, precision=HIGHEST_PREC) * jnp.exp(log_decay)[..., None]
    result = within_block + from_earlier + skip_in[:, None] * values_blk
    return result.reshape(series, length, head_count, width_p)

def reference(layer_input, head_input, out_grad, sensor_ids, valid_mask, sensor_table, proj_weight, step_bias, decay_log, skip_gain):
    pixel_count, length, model_d = layer_input.shape
    head_count = step_bias.shape[0]
    width_hp = head_input.shape[2]
    width_p = width_hp // head_count
    states_n = (proj_weight.shape[1] - head_count) // 2
    block_len = min(SPAN, length)
    is_second = (sensor_ids == 1)[None, :, None]
    sensor_embed = jnp.where(is_second, sensor_table[1], sensor_table[0])
    mixed_in = (layer_input.astype(jnp.float32) + sensor_embed).astype(jnp.bfloat16)
    flat_in = mixed_in.reshape(pixel_count * length, model_d)
    projected = jnp.dot(flat_in, proj_weight, preferred_element_type=jnp.float32).reshape(pixel_count, length, -1)
    pair_proj = projected[:, :, :2 * states_n].astype(jnp.bfloat16)
    step_pre = projected[:, :, 2 * states_n:] + step_bias
    valid_gate = valid_mask.astype(jnp.float32)[:, :, None]
    step_sizes = (valid_gate * jax.nn.softplus(step_pre)).astype(jnp.bfloat16)

    def local_scan(values_in, keys_in, reads_in, step_in, decay_in, skip_in):
        return span_scan(values_in, keys_in, reads_in, step_in, decay_in, skip_in, block_len)

    def one_group(group_item):
        group_values, cotangent, pair_blk, step_blk = group_item
        group_size = group_values.shape[0]
        _, pullback = jax.vjp(local_scan, group_values.astype(jnp.float32).reshape(group_size, length, head_count, width_p), pair_blk[..., :states_n].astype(jnp.float32), pair_blk[..., states_n:].astype(jnp.float32), step_blk.astype(jnp.float32), decay_log, skip_gain)
        grad_values, grad_b, grad_c, grad_steps, grad_decay, grad_skip = pullback(cotangent.astype(jnp.float32).reshape(group_size, length, head_count, width_p))
        return (grad_values.reshape(group_size, length, width_hp).astype(jnp.bfloat16), jnp.concatenate([grad_b, grad_c], axis=-1).astype(jnp.bfloat16), grad_steps.astype(jnp.bfloat16), grad_decay, grad_skip)

    def by_groups(array):
        return array.reshape((N_TILE, pixel_count // N_TILE) + array.shape[1:])
    results = lax.map(one_group, (by_groups(head_input), by_groups(out_grad), by_groups(pair_proj), by_groups(step_sizes)))
    value_grad = results[0].reshape(pixel_count, length, width_hp)
    pair_grad = results[1].reshape(pixel_count, length, 2 * states_n)
    step_grad = results[2].reshape(pixel_count, length, head_count)
    decay_part = lax.optimization_barrier(jnp.sum(results[3], axis=0))
    skip_part = lax.optimization_barrier(jnp.sum(results[4], axis=0))
    raw_grad = step_grad.astype(jnp.float32) * valid_gate * jax.nn.sigmoid(step_pre)
    proj_grad = jnp.concatenate([pair_grad, raw_grad.astype(jnp.bfloat16)], axis=-1).reshape(pixel_count * length, -1)
    grad_scale = 1.0 / math.sqrt(pixel_count * length)
    weight_grad = jnp.dot(flat_in.T, proj_grad, preferred_element_type=jnp.float32) * grad_scale
    flat_grad = jnp.dot(proj_grad, proj_weight.T, preferred_element_type=jnp.float32)
    input_grad = flat_grad.astype(jnp.bfloat16).reshape(pixel_count, length, model_d)
    flat_back = flat_grad.reshape(pixel_count, length, model_d)
    second_sum = lax.optimization_barrier(jnp.sum(jnp.where(is_second, flat_back, 0.0), axis=(0, 1)))
    first_sum = lax.optimization_barrier(jnp.sum(jnp.where(is_second, 0.0, flat_back), axis=(0, 1)))
    table_grad = jnp.stack([first_sum, second_sum]) * grad_scale
    head_grads = jnp.stack([decay_part, lax.optimization_barrier(jnp.sum(raw_grad, axis=(0, 1))), skip_part]) * grad_scale
    return (value_grad, input_grad, weight_grad, table_grad, head_grads)
```

```python
import math

import jax
import jax.numpy as jnp
from jax import lax
from jax.experimental import pallas as pl
from jax.experimental.pallas import tpu as pltpu
from jax.sharding import PartitionSpec as P

F32 = jnp.float32
BF16 = jnp.bfloat16
NEG_FILL = -1e30
NT = 64
RING = 8
LEN = 256


def mm(a, b, dims):
    return lax.dot_general(a, b, (dims, ((), ())), preferred_element_type=F32)


def iota(shape, dim):
    return lax.broadcasted_iota(jnp.int32, shape, dim)


def body(
    scale,
    li, xh, yh, ids, valid, table, wt, bias, decay, skip,
    vg, ig, wg, tg, hg,
    libuf, mix, wdt, gate, psend,
    pair, xb, yb, l_s, lt_s, dtt_s, g_s, dg_s, r_s, p_s, sk_s, dd_s, vs, pgs,
    pgr, igs, wfull, s0, r0, s1, r1, a1, s2, r2, s3, r3, q2, q1, p0,
    a0s, a0r, a1s, a1r, a2s, a2r, a3s, a3r, d4s, d4r,
    lsem, own_sem, ss, rs, fs, fr,
):
    tile = lax.axis_index("tile")
    me = lax.axis_index("date")
    core = lax.rem(me, 2)
    cx = lax.rem(me // 2, RING)
    zh = me // (2 * RING)
    cy = lax.rem(tile, RING)
    zl = tile // RING
    cz = zh * 2 + zl
    fi = (1 - core) * cx + core * cy
    se = core * cx + (1 - core) * cy

    def at(x, y, z, c):
        return (lax.rem(z, 2) * RING + y, ((z // 2) * RING + x) * 2 + c)

    def first_peer(f):
        return at((1 - core) * f + core * cx, core * f + (1 - core) * cy, cz, core)

    def second_peer(s):
        return at(core * s + (1 - core) * cx, (1 - core) * s + core * cy, cz, core)

    def x_peer(x):
        return at(x, cy, cz, core)

    def y_peer(y):
        return at(cx, y, cz, core)

    def z_peer(z):
        return at(cx, cy, z, core)

    partner = at(cx, cy, cz, 1 - core)

    def ring(n, mine, step):
        def one(k, carry):
            step(lax.rem(mine + k, n))
            return carry

        lax.fori_loop(1, n, one, 0)

    def send(src, dst, i, to, recv=None):
        pltpu.make_async_remote_copy(
            src_ref=src, dst_ref=dst, send_sem=ss.at[i], recv_sem=rs.at[i] if recv is None else recv,
            device_id=to, device_id_type=pl.DeviceIdType.MESH,
        ).start()

    def drain(ref, sem):
        pltpu.make_async_copy(ref, ref, sem).wait()

    barrier = pltpu.get_barrier_semaphore()

    def greet(to):
        pl.semaphore_signal(barrier, inc=1, device_id=to, device_id_type=pl.DeviceIdType.MESH)

    ring(NT, me, lambda d: greet((tile, d)))
    ring(RING, cy, lambda y: greet(y_peer(y)))

    def greet_z(k, carry):
        greet(at(cx, cy, 2 * k + 1 - zl, core))
        return carry

    lax.fori_loop(0, RING // 2, greet_z, 0)

    loads = [pltpu.make_async_copy(li.at[:, k], libuf.at[k], lsem.at[k]) for k in range(8)]
    for c in loads:
        c.start()
    own_x = pltpu.make_async_copy(xh.at[me], xb.at[:, me], own_sem.at[0])
    own_y = pltpu.make_async_copy(yh.at[me], yb.at[:, me], own_sem.at[1])
    own_x.start()
    own_y.start()
    row = iota((LEN, 128), 0)
    lane = iota((LEN, 128), 1)
    r3i = row & 3
    sens = jnp.where(r3i == 0, ids[0], jnp.where(r3i == 1, ids[1], jnp.where(r3i == 2, ids[2], ids[3])))
    is2 = sens == 1
    lif = libuf.reshape(8, LEN, 128)
    for k in range(8):
        loads[k].wait()
        cols = slice(128 * k, 128 * (k + 1))
        emb = jnp.where(is2, table[1:2, cols], table[0:1, cols])
        mix[:, cols] = (lif[k].astype(F32) + emb).astype(BF16)
    wdt[...] = jnp.zeros_like(wdt)
    wdt[0:8, :] = wt[256:264, :]
    pairs = mm(mix[...], wt[0:256, :], ((1,), (1,)))
    pre = mm(mix[...], wdt[...], ((1,), (1,)))
    lane1 = iota((1, 128), 1)
    bias_row = jnp.zeros((1, 128), F32)
    dec_row = jnp.zeros((1, 128), F32)
    for h in range(8):
        bias_row = jnp.where(lane1 == h, bias[h], bias_row)
        dec_row = jnp.where(lane1 == h, decay[h], dec_row)
    pre = pre + bias_row
    row6 = iota((LEN, NT), 0)
    col6 = iota((LEN, NT), 1)
    val = jnp.zeros((LEN, NT), F32)
    for t in range(4):
        val = jnp.where(((row6 >> 2) == col6) & ((row6 & 3) == t), valid[t : t + 1, :].astype(F32), val)
    val = jnp.sum(val, axis=1, keepdims=True)
    steps = jnp.where(lane < 8, val * jax.nn.softplus(pre), 0.0)
    gate[...] = jnp.where(lane < 8, val * jax.nn.sigmoid(pre), 0.0)
    psf = psend.reshape(3, LEN, 128)
    psf[0] = pairs[:, 0:128].astype(BF16)
    psf[1] = pairs[:, 128:256].astype(BF16)
    psf[2] = steps.astype(BF16)
    own_p = pltpu.make_async_copy(psend.at[:, me], pair.at[:, me], own_sem.at[2])
    own_p.start()

    pl.semaphore_wait(barrier, (NT - 1) + (RING - 1) + RING // 2)

    def forward(d):
        send(psend.at[:, d], pair.at[:, me], 0, (tile, d))
        send(yh.at[d], yb.at[:, me], 1, (tile, d))
        send(xh.at[d], xb.at[:, me], 2, (tile, d))

    ring(NT, me, forward)

    i2 = iota((LEN, LEN), 0)
    j2 = iota((LEN, LEN), 1)
    a_row = -jnp.exp(dec_row)
    row8 = iota((8, 128), 0)
    lane8 = iota((8, 128), 1)
    a_col = jnp.sum(jnp.where(row8 == lane8, a_row, 0.0), axis=1, keepdims=True)
    tril = (i2 >= j2).astype(F32).astype(BF16)
    strict = (i2 < j2).astype(F32).astype(BF16)
    eye = (i2 == j2).astype(F32).astype(BF16)
    dg_s[...] = jnp.zeros_like(dg_s)
    dd_s[...] = jnp.zeros_like(dd_s)

    own_p.wait()
    drain(pair.at[:, pl.ds(0, NT - 1)], rs.at[0])
    pf = pair.reshape(3, LEN, 128)
    dtb = pf[2]
    l_s[...] = mm(tril, dtb, ((1,), (0,))) * a_row
    lt_s[...] = mm(dtb, tril, ((0,), (1,)))[0:8, :] * a_col
    dtt_s[...] = mm(dtb, eye, ((0,), (0,)))[0:8, :]
    g_s[...] = mm(pf[1], pf[0], ((1,), (1,)))

    own_x.wait()
    own_y.wait()
    drain(yb.at[:, pl.ds(0, NT - 1)], rs.at[1])
    drain(xb.at[:, pl.ds(0, NT - 1)], rs.at[2])
    xf = xb.reshape(8, LEN, 128)
    yf = yb.reshape(8, LEN, 128)
    vf = vs.reshape(8, LEN, 128)

    def head(h, carry):
        pick = lane == h
        lc = jnp.sum(jnp.where(pick, l_s[...], 0.0), axis=1, keepdims=True)
        dtc = jnp.sum(jnp.where(pick, pf[2].astype(F32), 0.0), axis=1, keepdims=True)
        lr = lt_s[pl.ds(h, 1), :]
        dtr = dtt_s[pl.ds(h, 1), :]
        ker = jnp.exp(jnp.where(i2 >= j2, lc - lr, NEG_FILL))
        x = xf[h]
        y = yf[h]
        kz = ker * mm(y, x, ((1,), (1,)))
        dg_s[...] += kz * dtr
        g = g_s[...]
        both = kz * g
        p_s[pl.ds(h, 1), :] = jnp.sum(both, axis=0, keepdims=True)
        spread = mm((both * dtr).astype(BF16), strict, ((1,), (0,)))
        r_s[pl.ds(h, 1), :] = jnp.sum(jnp.where(i2 >= j2, spread, 0.0), axis=0, keepdims=True)
        dw = mm((ker * g).astype(BF16), y, ((0,), (0,)))
        y32 = y.astype(F32)
        vf[h] = (dw * dtc + skip[h] * y32).astype(BF16)
        sk_s[pl.ds(h, 1), :] = jnp.sum(y32 * x.astype(F32), axis=0, keepdims=True)
        return carry

    lax.fori_loop(0, 8, head, 0)
    pgf = pgs.reshape(3, LEN, 128)
    dgb = dg_s[...].astype(BF16)
    pgf[0] = mm(dgb, pf[1], ((0,), (0,))).astype(BF16)
    pgf[1] = mm(dgb, pf[0], ((1,), (0,))).astype(BF16)
    dd_s[0:8, :] = a_col * r_s[...] + p_s[...]
    pgf[2] = jnp.transpose(dd_s[...]).astype(BF16)
    own_g = pltpu.make_async_copy(pgs.at[:, me], pgr.at[:, me], own_sem.at[3])
    own_g.start()
    ring(NT, me, lambda d: send(pgs.at[:, d], pgr.at[:, me], 3, (tile, d)))
    own_v = pltpu.make_async_copy(vs.at[:, me], vg.at[me], own_sem.at[4])
    own_v.start()
    ring(NT, me, lambda d: send(vs.at[:, d], vg.at[me], 4, (tile, d)))
    decay_col = a_col * jnp.sum(r_s[...] * dtt_s[...], axis=1, keepdims=True)
    skip_col = jnp.sum(sk_s[...], axis=1, keepdims=True)
    head_row = jnp.sum(
        jnp.where(lane8 == row8, decay_col, 0.0) + jnp.where(lane8 == row8 + 64, skip_col, 0.0), axis=0, keepdims=True
    )

    own_g.wait()
    drain(pgr.at[:, pl.ds(0, NT - 1)], rs.at[3])
    prf = pgr.reshape(3, LEN, 128)
    raw = prf[2].astype(F32) * gate[...]
    rawb = raw.astype(BF16)
    gb = prf[0]
    gc = prf[1]
    wb = mm(gb, mix[...], ((0,), (0,)))
    wc = mm(gc, mix[...], ((0,), (0,)))
    for k in range(8):
        cols = slice(128 * k, 128 * (k + 1))
        wfull[0, k] = wb[:, cols]
        wfull[1, k] = wc[:, cols]
    s0[...] = wfull[1 - core].astype(BF16)
    send(s0, r0, 5, partner)
    wd = mm(rawb, mix[...], ((0,), (0,)))
    for k in range(8):
        a0s[k] = wd[0:8, 128 * k : 128 * (k + 1)]
    tok = iota((8, LEN), 1) & 3
    sens8 = jnp.where(tok == 0, ids[0], jnp.where(tok == 1, ids[1], jnp.where(tok == 2, ids[2], ids[3])))
    rows8 = iota((8, LEN), 0)
    sel = jnp.where(rows8 < 3, (sens8 != 1).astype(F32), jnp.where(rows8 < 6, (sens8 == 1).astype(F32), 0.0)).astype(BF16)
    sum_b = mm(sel, gb, ((1,), (0,)))
    sum_c = mm(sel, gc, ((1,), (0,)))
    sum_r = mm(sel, rawb, ((1,), (0,)))
    raw_sum = jnp.sum(raw, axis=0, keepdims=True)
    kind = jnp.where(row8 < 3, row8, row8 - 3)
    small = jnp.where(kind == 0, sum_b, jnp.where(kind == 1, sum_c, sum_r))
    small = jnp.where(row8 == 6, head_row, jnp.where(row8 == 7, raw_sum, small))
    a0s[8] = small
    send(a0s, a0r, 6, partner)

    drain(r0, rs.at[5])
    for k in range(8):
        both = wfull[core, k] + r0[k].astype(F32)
        wfull[core, k] = both
        s1[k] = both.astype(BF16)
    ring(RING, fi, lambda f: send(s1.at[f], r1.at[fi], 7, first_peer(f)))
    drain(a0r, rs.at[6])
    for k in range(8):
        a1s[k, 0] = a0s[k] + a0r[k]
        a1s[k, 1] = a0s[8] + a0r[8]
    a1r[cx] = a1s[cx]
    ring(RING, cx, lambda x: send(a1s.at[x], a1r.at[cx], 8, x_peer(x)))

    flat = mm(gb, wt[0:128, :], ((1,), (0,))) + mm(gc, wt[128:256, :], ((1,), (0,))) + mm(rawb, wdt[...], ((1,), (0,)))
    igf = igs.reshape(8, LEN, 128)
    for k in range(8):
        igf[k] = flat[:, 128 * k : 128 * (k + 1)].astype(BF16)
    stores = [pltpu.make_async_copy(igs.at[k], ig.at[:, k], lsem.at[k]) for k in range(8)]
    for c in stores:
        c.start()

    drain(r1.at[pl.ds(0, RING - 1)], rs.at[7])
    a1[...] = wfull[core, fi]

    def add1(k, carry):
        a1[...] += r1[lax.rem(fi + k, RING)].astype(F32)
        return carry

    lax.fori_loop(1, RING, add1, 0)
    s2[...] = a1[...].astype(BF16).reshape(RING, 16, 128)
    ring(RING, se, lambda s: send(s2.at[s], r2.at[se], 9, second_peer(s)))
    drain(a1r.at[pl.ds(0, RING - 1)], rs.at[8])
    a2s[...] = ((a1r[0] + a1r[1]) + (a1r[2] + a1r[3])) + ((a1r[4] + a1r[5]) + (a1r[6] + a1r[7]))
    a2r[cy] = a2s[...]
    ring(RING, cy, lambda y: send(a2s, a2r.at[cy], 10, y_peer(y)))

    drain(r2.at[pl.ds(0, RING - 1)], rs.at[9])
    s3[...] = a1[pl.ds(pl.multiple_of(se * 16, 16), 16), :]

    def add2(k, carry):
        s3[...] += r2[lax.rem(se + k, RING)].astype(F32)
        return carry

    lax.fori_loop(1, RING, add2, 0)
    r3[cz] = s3[...]
    ring(RING, cz, lambda z: send(s3, r3.at[cz], 11, z_peer(z)))
    drain(a2r.at[pl.ds(0, RING - 1)], rs.at[10])
    a3s[...] = ((a2r[0] + a2r[1]) + (a2r[2] + a2r[3])) + ((a2r[4] + a2r[5]) + (a2r[6] + a2r[7]))
    a3r[cz] = a3s[...]
    ring(RING, cz, lambda z: send(a3s, a3r.at[cz], 12, z_peer(z)))

    drain(r3.at[pl.ds(0, RING - 1)], rs.at[11])
    total = ((r3[0] + r3[1]) + (r3[2] + r3[3])) + ((r3[4] + r3[5]) + (r3[6] + r3[7]))
    q2[se] = (total * scale).astype(BF16)
    ring(RING, se, lambda s: send(q2.at[se], q2.at[se], 13, second_peer(s)))
    drain(a3r.at[pl.ds(0, RING - 1)], rs.at[12])
    aux = ((a3r[0] + a3r[1]) + (a3r[2] + a3r[3])) + ((a3r[4] + a3r[5]) + (a3r[6] + a3r[7]))
    aux = aux * scale
    d4s[...] = aux[0]
    d4r[cx] = aux[0]
    ring(RING, cx, lambda x: send(d4s, d4r.at[cx], 14, x_peer(x)))
    small = aux[1]

    drain(q2.at[pl.ds(0, RING - 1)], rs.at[13])
    send(q2, p0.at[fi], 15, partner, fr.at[fi])
    ring(RING, fi, lambda f: send(q2, q1.at[fi], 16, first_peer(f), fs.at[fi]))
    q1[fi] = q2[...]

    hi = small.astype(BF16)
    left = small - hi.astype(F32)
    mid = left.astype(BF16)
    low = (left - mid.astype(F32)).astype(BF16)

    def times(w):
        return mm(hi, w, ((1,), (0,))) + (mm(mid, w, ((1,), (0,))) + mm(low, w, ((1,), (0,))))

    tb = times(wt[0:128, :])
    tc = times(wt[128:256, :])
    tr = times(wdt[...])
    tg[0:1, :] = tb[0:1] + tc[1:2] + tr[2:3]
    tg[1:2, :] = tb[3:4] + tc[4:5] + tr[5:6]
    hg[0:1, :] = small[6:7, 0:8]
    hg[1:2, :] = small[7:8, 0:8]
    hg[2:3, :] = pltpu.roll(small, 64, 1)[6:7, 0:8]
    drain(d4r.at[pl.ds(0, RING - 1)], rs.at[14])
    for k in range(8):
        wg[256:264, 128 * k : 128 * (k + 1)] = d4r[k]

    def pass_on(f):
        drain(q1.at[f], fs.at[f])
        send(q1.at[f], p0.at[f], 15, partner, fr.at[f])

    ring(RING, fi, pass_on)
    mine = pl.multiple_of(core * 128, 128)
    other = pl.multiple_of((1 - core) * 128, 128)
    for k in range(8):
        wg[pl.ds(mine, 128), 128 * k : 128 * (k + 1)] = q1[k].reshape(128, 128).astype(F32)
    for k in range(8):
        drain(p0.at[k], fr.at[k])
        wg[pl.ds(other, 128), 128 * k : 128 * (k + 1)] = p0[k].reshape(128, 128).astype(F32)

    own_v.wait()
    drain(vs.at[:, pl.ds(0, NT - 1)], rs.at[4])
    for c in stores:
        c.wait()
    drain(psend.at[:, pl.ds(0, NT - 1)], ss.at[0])
    drain(yb.at[:, pl.ds(0, NT - 1)], ss.at[1])
    drain(xb.at[:, pl.ds(0, NT - 1)], ss.at[2])
    drain(pgs.at[:, pl.ds(0, NT - 1)], ss.at[3])
    drain(vs.at[:, pl.ds(0, NT - 1)], ss.at[4])
    drain(s0, ss.at[5])
    drain(a0s, ss.at[6])
    drain(s1.at[pl.ds(0, RING - 1)], ss.at[7])
    drain(a1s.at[pl.ds(0, RING - 1)], ss.at[8])
    drain(s2.at[pl.ds(0, RING - 1)], ss.at[9])
    drain(a2r.at[pl.ds(0, RING - 1)], ss.at[10])
    drain(r3.at[pl.ds(0, RING - 1)], ss.at[11])
    drain(a3r.at[pl.ds(0, RING - 1)], ss.at[12])
    drain(q2.at[pl.ds(0, RING - 1)], ss.at[13])
    drain(d4r.at[pl.ds(0, RING - 1)], ss.at[14])
    drain(p0, ss.at[15])
    drain(q1.at[pl.ds(0, RING - 1)], ss.at[16])


def on_device(layer_input, head_input, out_grad, sensor_ids, valid_mask, sensor_table, proj_weight, step_bias, decay_log, skip_gain):
    pixels, dates, width = layer_input.shape
    total = pixels * dates * lax.axis_size("tile") * lax.axis_size("date")

    def heads(a):
        return a.reshape(pixels, dates, 8, 128).transpose(0, 2, 1, 3)

    any_ = pl.BlockSpec(memory_space=pl.ANY)
    vm = pl.BlockSpec(memory_space=pltpu.VMEM)
    sm = pl.BlockSpec(memory_space=pltpu.SMEM)
    four = (8, NT, 4, 128)

    def v(shape, dtype):
        return pltpu.VMEM(shape, dtype)

    scratch = [
        v(four, BF16), v((LEN, 1024), BF16), v((128, 1024), BF16), v((LEN, 128), F32), v((3, NT, 4, 128), BF16),
        v((3, NT, 4, 128), BF16), v(four, BF16), v(four, BF16), v((LEN, 128), F32), v((8, LEN), F32), v((8, LEN), F32),
        v((LEN, LEN), F32), v((LEN, LEN), F32), v((8, LEN), F32), v((8, LEN), F32), v((8, 128), F32), v((128, LEN), F32),
        v(four, BF16), v((3, NT, 4, 128), BF16),
        v((3, NT, 4, 128), BF16), v(four, BF16), v((2, 8, 128, 128), F32), v((8, 128, 128), BF16), v((8, 128, 128), BF16),
        v((8, 128, 128), BF16), v((8, 128, 128), BF16), v((128, 128), F32), v((8, 16, 128), BF16), v((8, 16, 128), BF16),
        v((16, 128), F32), v((8, 16, 128), F32), v((8, 16, 128), BF16), v((8, 8, 16, 128), BF16), v((8, 8, 16, 128), BF16),
        v((9, 8, 128), F32), v((9, 8, 128), F32), v((8, 2, 8, 128), F32), v((8, 2, 8, 128), F32), v((2, 8, 128), F32),
        v((8, 2, 8, 128), F32), v((2, 8, 128), F32), v((8, 2, 8, 128), F32), v((8, 128), F32), v((8, 8, 128), F32),
        pltpu.SemaphoreType.DMA((8,)), pltpu.SemaphoreType.DMA((5,)), pltpu.SemaphoreType.DMA((17,)),
        pltpu.SemaphoreType.DMA((15,)), pltpu.SemaphoreType.DMA((8,)), pltpu.SemaphoreType.DMA((8,)),
    ]

    def kernel(*refs):
        body(1.0 / math.sqrt(total), *refs)

    vg, ig, wg, tg, hg = pl.pallas_call(
        kernel,
        name="mixer_backward",
        out_shape=(
            jax.ShapeDtypeStruct((pixels, 8, dates, 128), BF16),
            jax.ShapeDtypeStruct((pixels, 8, dates, 128), BF16),
            jax.ShapeDtypeStruct((264, 1024), F32),
            jax.ShapeDtypeStruct((2, 1024), F32),
            jax.ShapeDtypeStruct((3, 8), F32),
        ),
        in_specs=[any_, any_, any_, sm, vm, vm, vm, sm, sm, sm],
        out_specs=(any_, any_, vm, vm, vm),
        scratch_shapes=scratch,
        compiler_params=pltpu.CompilerParams(collective_id=0, has_side_effects=True),
    )(
        heads(layer_input), heads(head_input), heads(out_grad), sensor_ids, valid_mask.T, sensor_table, proj_weight.T,
        step_bias, decay_log, skip_gain,
    )

    def dates_first(a):
        return a.transpose(0, 2, 1, 3).reshape(pixels, dates, width)

    return dates_first(vg), dates_first(ig), wg.T, tg, hg


def solution(mesh):
    in_specs = (
        P("tile", "date", None), P("tile", "date", None), P("tile", "date", None), P("date"), P("tile", "date"),
        P(), P(), P(), P(), P(),
    )
    out_specs = (P("tile", "date", None), P("tile", "date", None), P(), P(), P())
    return jax.shard_map(on_device, mesh=mesh, in_specs=in_specs, out_specs=out_specs, check_vma=False)
```

```python
import math

import jax
import jax.numpy as jnp
from jax import lax
from jax.experimental import pallas as pl
from jax.experimental.pallas import tpu as pltpu
from jax.sharding import PartitionSpec as P

F32 = jnp.float32
BF16 = jnp.bfloat16
NEG_FILL = -1e30
NT = 64
RING = 8
EARLY = 6
OWN = 46
LEN = 256


def mm(a, b, dims):
    return lax.dot_general(a, b, (dims, ((), ())), preferred_element_type=F32)


def iota(shape, dim):
    return lax.broadcasted_iota(jnp.int32, shape, dim)


def body(
    scale,
    li, xh, yh, ids_h, valid_h, table_h, wt_h, bias_h, decay_h, skip_h,
    vg, ig, wg, tg, hg,
    ids, valid, table, wt, bias, decay, skip,
    libuf, mix, wdt, gate, psend,
    pair, xb, yb, l_s, lt_s, dtt_s, g_s, dg_s, r_s, p_s, sk_s, dd_s, vs, pgs,
    pgr, wfull, s0, r0, s1, r1, a1, s2, r2, s3, r3, q2, q1, p0,
    a0s, a0r, a1s, a1r, a2s, a2r, a3s, a3r, d4s, d4r,
    in_sem, lsem, own_sem, ss, rs, fs, fr,
):
    tile = lax.axis_index("tile")
    me = lax.axis_index("date")
    core = lax.rem(me, 2)
    cx = lax.rem(me // 2, RING)
    zh = me // (2 * RING)
    cy = lax.rem(tile, RING)
    zl = tile // RING
    cz = zh * 2 + zl
    fi = (1 - core) * cx + core * cy
    se = core * cx + (1 - core) * cy

    def at(x, y, z, c):
        return (lax.rem(z, 2) * RING + y, ((z // 2) * RING + x) * 2 + c)

    def first_peer(f):
        return at((1 - core) * f + core * cx, core * f + (1 - core) * cy, cz, core)

    def second_peer(s):
        return at(core * s + (1 - core) * cx, (1 - core) * s + core * cy, cz, core)

    def x_peer(x):
        return at(x, cy, cz, core)

    def y_peer(y):
        return at(cx, y, cz, core)

    def z_peer(z):
        return at(cx, cy, z, core)

    partner = at(cx, cy, cz, 1 - core)

    def ring(n, mine, step):
        def one(k, carry):
            step(lax.rem(mine + k, n))
            return carry

        lax.fori_loop(1, n, one, 0)

    def offset(n):
        return ((n + 1) // 2) * (1 - 2 * lax.rem(n, 2))

    def far_first(low, high, step):
        def one(k, carry):
            v = lax.rem(k // 2, 4)
            u = lax.rem(k // 8 + 2 * RING - 2 * v, RING)
            z = lax.rem(zh + 2 + offset(v) + 4, 4)
            x = lax.rem(cx + RING // 2 + offset(u) + RING, RING)
            step((z * RING + x) * 2 + lax.rem(core + k, 2))
            return carry

        for a, b in ((low, min(high, OWN)), (max(low, OWN + 1), high)):
            if a < b:
                lax.fori_loop(a, b, one, 0)

    def send(src, dst, i, to, recv=None):
        pltpu.make_async_remote_copy(
            src_ref=src, dst_ref=dst, send_sem=ss.at[i], recv_sem=rs.at[i] if recv is None else recv,
            device_id=to, device_id_type=pl.DeviceIdType.MESH,
        ).start()

    def drain(ref, sem):
        pltpu.make_async_copy(ref, ref, sem).wait()

    barrier = pltpu.get_barrier_semaphore()

    def greet(to):
        pl.semaphore_signal(barrier, inc=1, device_id=to, device_id_type=pl.DeviceIdType.MESH)

    far_first(0, NT, lambda d: greet((tile, d)))
    ring(RING, cy, lambda y: greet(y_peer(y)))

    def greet_z(k, carry):
        greet(at(cx, cy, 2 * k + 1 - zl, core))
        return carry

    lax.fori_loop(0, RING // 2, greet_z, 0)

    smalls = [
        pltpu.make_async_copy(a, b, in_sem.at[i])
        for i, (a, b) in enumerate((
            (ids_h, ids), (valid_h, valid), (table_h, table), (wt_h, wt), (bias_h, bias), (decay_h, decay), (skip_h, skip),
        ))
    ]
    for c in smalls:
        c.start()
    loads = [pltpu.make_async_copy(li.at[:, k], libuf.at[k], lsem.at[k]) for k in range(8)]
    for c in loads:
        c.start()
    own_x = pltpu.make_async_copy(xh.at[me], xb.at[:, me], own_sem.at[0])
    own_y = pltpu.make_async_copy(yh.at[me], yb.at[:, me], own_sem.at[1])
    own_x.start()
    own_y.start()
    pl.semaphore_wait(barrier, (NT - 1) + (RING - 1) + RING // 2)
    far_first(0, NT, lambda d: send(yh.at[d], yb.at[:, me], 1, (tile, d)))

    for c in smalls:
        c.wait()
    row = iota((LEN, 128), 0)
    lane = iota((LEN, 128), 1)
    r3i = row & 3
    sens = jnp.where(r3i == 0, ids[0], jnp.where(r3i == 1, ids[1], jnp.where(r3i == 2, ids[2], ids[3])))
    is2 = sens == 1
    lif = libuf.reshape(8, LEN, 128)
    for k in range(8):
        loads[k].wait()
        cols = slice(128 * k, 128 * (k + 1))
        emb = jnp.where(is2, table[1:2, cols], table[0:1, cols])
        mix[:, cols] = (lif[k].astype(F32) + emb).astype(BF16)
    wdt[...] = jnp.zeros_like(wdt)
    wdt[0:8, :] = wt[256:264, :]
    pairs = mm(mix[...], wt[0:256, :], ((1,), (1,)))
    pre = mm(mix[...], wdt[...], ((1,), (1,)))
    lane1 = iota((1, 128), 1)
    bias_row = jnp.zeros((1, 128), F32)
    dec_row = jnp.zeros((1, 128), F32)
    for h in range(8):
        bias_row = jnp.where(lane1 == h, bias[h], bias_row)
        dec_row = jnp.where(lane1 == h, decay[h], dec_row)
    pre = pre + bias_row
    row6 = iota((LEN, NT), 0)
    col6 = iota((LEN, NT), 1)
    val = jnp.zeros((LEN, NT), F32)
    for t in range(4):
        val = jnp.where(((row6 >> 2) == col6) & ((row6 & 3) == t), valid[t : t + 1, :].astype(F32), val)
    val = jnp.sum(val, axis=1, keepdims=True)
    steps = jnp.where(lane < 8, val * jax.nn.softplus(pre), 0.0)
    gate[...] = jnp.where(lane < 8, val * jax.nn.sigmoid(pre), 0.0)
    psf = psend.reshape(3, LEN, 128)
    psf[0] = pairs[:, 0:128].astype(BF16)
    psf[1] = pairs[:, 128:256].astype(BF16)
    psf[2] = steps.astype(BF16)
    own_p = pltpu.make_async_copy(psend.at[:, me], pair.at[:, me], own_sem.at[2])
    own_p.start()

    far_first(0, NT, lambda d: send(psend.at[:, d], pair.at[:, me], 0, (tile, d)))
    far_first(0, NT, lambda d: send(xh.at[d, pl.ds(0, EARLY)], xb.at[pl.ds(0, EARLY), me], 2, (tile, d)))
    far_first(0, NT, lambda d: send(xh.at[d, pl.ds(EARLY, 8 - EARLY)], xb.at[pl.ds(EARLY, 8 - EARLY), me], 17, (tile, d)))

    i2 = iota((LEN, LEN), 0)
    j2 = iota((LEN, LEN), 1)
    a_row = -jnp.exp(dec_row)
    row8 = iota((8, 128), 0)
    lane8 = iota((8, 128), 1)
    a_col = jnp.sum(jnp.where(row8 == lane8, a_row, 0.0), axis=1, keepdims=True)
    tril = (i2 >= j2).astype(F32).astype(BF16)
    strict = (i2 < j2).astype(F32).astype(BF16)
    eye = (i2 == j2).astype(F32).astype(BF16)
    dg_s[...] = jnp.zeros_like(dg_s)
    dd_s[...] = jnp.zeros_like(dd_s)

    own_p.wait()
    drain(pair.at[:, pl.ds(0, NT - 1)], rs.at[0])
    pf = pair.reshape(3, LEN, 128)
    dtb = pf[2]
    l_s[...] = mm(tril, dtb, ((1,), (0,))) * a_row
    lt_s[...] = mm(dtb, tril, ((0,), (1,)))[0:8, :] * a_col
    dtt_s[...] = mm(dtb, eye, ((0,), (0,)))[0:8, :]
    g_s[...] = mm(pf[1], pf[0], ((1,), (1,)))

    own_x.wait()
    own_y.wait()
    drain(yb.at[:, pl.ds(0, NT - 1)], rs.at[1])
    drain(xb.at[pl.ds(0, EARLY), pl.ds(0, NT - 1)], rs.at[2])
    xf = xb.reshape(8, LEN, 128)
    yf = yb.reshape(8, LEN, 128)
    vf = vs.reshape(8, LEN, 128)

    def head(h, carry):
        pick = lane == h
        lc = jnp.sum(jnp.where(pick, l_s[...], 0.0), axis=1, keepdims=True)
        dtc = jnp.sum(jnp.where(pick, pf[2].astype(F32), 0.0), axis=1, keepdims=True)
        lr = lt_s[pl.ds(h, 1), :]
        dtr = dtt_s[pl.ds(h, 1), :]
        ker = jnp.exp(jnp.where(i2 >= j2, lc - lr, NEG_FILL))
        x = xf[h]
        y = yf[h]
        kz = ker * mm(y, x, ((1,), (1,)))
        dg_s[...] += kz * dtr
        g = g_s[...]
        both = kz * g
        p_s[pl.ds(h, 1), :] = jnp.sum(both, axis=0, keepdims=True)
        spread = mm((both * dtr).astype(BF16), strict, ((1,), (0,)))
        r_s[pl.ds(h, 1), :] = jnp.sum(jnp.where(i2 >= j2, spread, 0.0), axis=0, keepdims=True)
        dw = mm((ker * g).astype(BF16), y, ((0,), (0,)))
        y32 = y.astype(F32)
        vf[h] = (dw * dtc + skip[h] * y32).astype(BF16)
        sk_s[pl.ds(h, 1), :] = jnp.sum(y32 * x.astype(F32), axis=0, keepdims=True)
        return carry

    lax.fori_loop(0, EARLY, head, 0)
    drain(xb.at[pl.ds(EARLY, 8 - EARLY), pl.ds(0, NT - 1)], rs.at[17])
    lax.fori_loop(EARLY, 8, head, 0)
    pgf = pgs.reshape(3, LEN, 128)
    dgb = dg_s[...].astype(BF16)
    pgf[0] = mm(dgb, pf[1], ((0,), (0,))).astype(BF16)
    pgf[1] = mm(dgb, pf[0], ((1,), (0,))).astype(BF16)
    dd_s[0:8, :] = a_col * r_s[...] + p_s[...]
    pgf[2] = jnp.transpose(dd_s[...]).astype(BF16)
    own_g = pltpu.make_async_copy(pgs.at[:, me], pgr.at[:, me], own_sem.at[3])
    own_g.start()
    far_first(0, NT, lambda d: send(pgs.at[:, d], pgr.at[:, me], 3, (tile, d)))
    own_v = pltpu.make_async_copy(vs.at[:, me], vg.at[me], own_sem.at[4])
    own_v.start()

    def give_values(low, high):
        far_first(low, high, lambda d: send(vs.at[:, d], vg.at[me], 4, (tile, d)))

    give_values(0, 28)
    decay_col = a_col * jnp.sum(r_s[...] * dtt_s[...], axis=1, keepdims=True)
    skip_col = jnp.sum(sk_s[...], axis=1, keepdims=True)
    head_row = jnp.sum(
        jnp.where(lane8 == row8, decay_col, 0.0) + jnp.where(lane8 == row8 + 64, skip_col, 0.0), axis=0, keepdims=True
    )

    own_g.wait()
    drain(pgr.at[:, pl.ds(0, NT - 1)], rs.at[3])
    prf = pgr.reshape(3, LEN, 128)
    raw = prf[2].astype(F32) * gate[...]
    rawb = raw.astype(BF16)
    gb = prf[0]
    gc = prf[1]
    give = mm(prf[1 - core], mix[...], ((0,), (0,)))
    for k in range(8):
        s0[k] = give[:, 128 * k : 128 * (k + 1)].astype(BF16)
    send(s0, r0, 5, partner)
    keep = mm(prf[core], mix[...], ((0,), (0,)))
    for k in range(8):
        wfull[k] = keep[:, 128 * k : 128 * (k + 1)]
    wd = mm(rawb, mix[...], ((0,), (0,)))
    for k in range(8):
        a0s[k] = wd[0:8, 128 * k : 128 * (k + 1)]
    tok = iota((8, LEN), 1) & 3
    sens8 = jnp.where(tok == 0, ids[0], jnp.where(tok == 1, ids[1], jnp.where(tok == 2, ids[2], ids[3])))
    rows8 = iota((8, LEN), 0)
    sel = jnp.where(rows8 < 3, (sens8 != 1).astype(F32), jnp.where(rows8 < 6, (sens8 == 1).astype(F32), 0.0)).astype(BF16)
    sum_b = mm(sel, gb, ((1,), (0,)))
    sum_c = mm(sel, gc, ((1,), (0,)))
    sum_r = mm(sel, rawb, ((1,), (0,)))
    raw_sum = jnp.sum(raw, axis=0, keepdims=True)
    kind = jnp.where(row8 < 3, row8, row8 - 3)
    small = jnp.where(kind == 0, sum_b, jnp.where(kind == 1, sum_c, sum_r))
    small = jnp.where(row8 == 6, head_row, jnp.where(row8 == 7, raw_sum, small))
    a0s[8] = small
    send(a0s, a0r, 6, partner)

    drain(r0, rs.at[5])
    for k in range(8):
        both = wfull[k] + r0[k].astype(F32)
        wfull[k] = both
        s1[k] = both.astype(BF16)
    ring(RING, fi, lambda f: send(s1.at[f], r1.at[fi], 7, first_peer(f)))
    drain(a0r, rs.at[6])
    for k in range(8):
        a1s[k, 0] = a0s[k] + a0r[k]
        a1s[k, 1] = a0s[8] + a0r[8]
    a1r[cx] = a1s[cx]
    ring(RING, cx, lambda x: send(a1s.at[x], a1r.at[cx], 8, x_peer(x)))

    igf = ig.reshape(8, LEN, 128)

    def input_grad(low, high):
        for k in range(low, high):
            cols = slice(128 * k, 128 * (k + 1))
            flat = mm(gb, wt[0:128, cols], ((1,), (0,))) + mm(gc, wt[128:256, cols], ((1,), (0,)))
            igf[k] = (flat + mm(rawb, wdt[:, cols], ((1,), (0,)))).astype(BF16)

    input_grad(0, 2)

    drain(r1.at[pl.ds(0, RING - 1)], rs.at[7])
    a1[...] = wfull[fi]

    def add1(k, carry):
        a1[...] += r1[lax.rem(fi + k, RING)].astype(F32)
        return carry

    lax.fori_loop(1, RING, add1, 0)
    s2[...] = a1[...].astype(BF16).reshape(RING, 16, 128)
    ring(RING, se, lambda s: send(s2.at[s], r2.at[se], 9, second_peer(s)))
    drain(a1r.at[pl.ds(0, RING - 1)], rs.at[8])
    a2s[...] = ((a1r[0] + a1r[1]) + (a1r[2] + a1r[3])) + ((a1r[4] + a1r[5]) + (a1r[6] + a1r[7]))
    a2r[cy] = a2s[...]
    ring(RING, cy, lambda y: send(a2s, a2r.at[cy], 10, y_peer(y)))
    give_values(28, 40)
    input_grad(2, 4)

    drain(r2.at[pl.ds(0, RING - 1)], rs.at[9])
    s3[...] = a1[pl.ds(pl.multiple_of(se * 16, 16), 16), :]

    def add2(k, carry):
        s3[...] += r2[lax.rem(se + k, RING)].astype(F32)
        return carry

    lax.fori_loop(1, RING, add2, 0)
    r3[cz] = s3[...]
    ring(RING, cz, lambda z: send(s3, r3.at[cz], 11, z_peer(z)))
    drain(a2r.at[pl.ds(0, RING - 1)], rs.at[10])
    a3s[...] = ((a2r[0] + a2r[1]) + (a2r[2] + a2r[3])) + ((a2r[4] + a2r[5]) + (a2r[6] + a2r[7]))
    a3r[cz] = a3s[...]
    ring(RING, cz, lambda z: send(a3s, a3r.at[cz], 12, z_peer(z)))
    give_values(40, 52)
    input_grad(4, 6)

    drain(r3.at[pl.ds(0, RING - 1)], rs.at[11])
    total = ((r3[0] + r3[1]) + (r3[2] + r3[3])) + ((r3[4] + r3[5]) + (r3[6] + r3[7]))
    q2[se] = (total * scale).astype(BF16)
    ring(RING, se, lambda s: send(q2.at[se], q2.at[se], 13, second_peer(s)))
    drain(a3r.at[pl.ds(0, RING - 1)], rs.at[12])
    aux = ((a3r[0] + a3r[1]) + (a3r[2] + a3r[3])) + ((a3r[4] + a3r[5]) + (a3r[6] + a3r[7]))
    aux = aux * scale
    d4s[...] = aux[0]
    d4r[cx] = aux[0]
    ring(RING, cx, lambda x: send(d4s, d4r.at[cx], 14, x_peer(x)))
    give_values(52, NT)
    input_grad(6, 8)
    small = aux[1]

    drain(q2.at[pl.ds(0, RING - 1)], rs.at[13])
    send(q2, p0.at[fi], 15, partner, fr.at[fi])
    ring(RING, fi, lambda f: send(q2, q1.at[fi], 16, first_peer(f), fs.at[fi]))
    q1[fi] = q2[...]

    hi = small.astype(BF16)
    left = small - hi.astype(F32)
    mid = left.astype(BF16)
    low = (left - mid.astype(F32)).astype(BF16)

    def times(w):
        return mm(hi, w, ((1,), (0,))) + (mm(mid, w, ((1,), (0,))) + mm(low, w, ((1,), (0,))))

    tb = times(wt[0:128, :])
    tc = times(wt[128:256, :])
    tr = times(wdt[...])
    tg[0:1, :] = tb[0:1] + tc[1:2] + tr[2:3]
    tg[1:2, :] = tb[3:4] + tc[4:5] + tr[5:6]
    hg[0:1, :] = small[6:7, 0:8]
    hg[1:2, :] = small[7:8, 0:8]
    hg[2:3, :] = pltpu.roll(small, 64, 1)[6:7, 0:8]
    drain(d4r.at[pl.ds(0, RING - 1)], rs.at[14])
    for k in range(8):
        wg[256:264, 128 * k : 128 * (k + 1)] = d4r[k]

    def pass_on(f):
        drain(q1.at[f], fs.at[f])
        send(q1.at[f], p0.at[f], 15, partner, fr.at[f])

    ring(RING, fi, pass_on)
    mine = pl.multiple_of(core * 128, 128)
    other = pl.multiple_of((1 - core) * 128, 128)
    for k in range(8):
        wg[pl.ds(mine, 128), 128 * k : 128 * (k + 1)] = q1[k].reshape(128, 128).astype(F32)
    for k in range(8):
        drain(p0.at[k], fr.at[k])
        wg[pl.ds(other, 128), 128 * k : 128 * (k + 1)] = p0[k].reshape(128, 128).astype(F32)

    own_v.wait()
    drain(vs.at[:, pl.ds(0, NT - 1)], rs.at[4])
    drain(psend.at[:, pl.ds(0, NT - 1)], ss.at[0])
    drain(yb.at[:, pl.ds(0, NT - 1)], ss.at[1])
    drain(xb.at[pl.ds(0, EARLY), pl.ds(0, NT - 1)], ss.at[2])
    drain(xb.at[pl.ds(EARLY, 8 - EARLY), pl.ds(0, NT - 1)], ss.at[17])
    drain(pgs.at[:, pl.ds(0, NT - 1)], ss.at[3])
    drain(vs.at[:, pl.ds(0, NT - 1)], ss.at[4])
    drain(s0, ss.at[5])
    drain(a0s, ss.at[6])
    drain(s1.at[pl.ds(0, RING - 1)], ss.at[7])
    drain(a1s.at[pl.ds(0, RING - 1)], ss.at[8])
    drain(s2.at[pl.ds(0, RING - 1)], ss.at[9])
    drain(a2r.at[pl.ds(0, RING - 1)], ss.at[10])
    drain(r3.at[pl.ds(0, RING - 1)], ss.at[11])
    drain(a3r.at[pl.ds(0, RING - 1)], ss.at[12])
    drain(q2.at[pl.ds(0, RING - 1)], ss.at[13])
    drain(d4r.at[pl.ds(0, RING - 1)], ss.at[14])
    drain(p0, ss.at[15])
    drain(q1.at[pl.ds(0, RING - 1)], ss.at[16])


def write_out(vi, ii, wi, ti, hi, vo, io, wo, to, ho, sem):
    pieces = [(vi.at[pl.ds(16 * n, 16)], vo.at[pl.ds(16 * n, 16)]) for n in range(4)]
    pieces += [(ii.at[k], io.at[:, k]) for k in range(8)]
    pieces += [(wi.at[pl.ds(88 * n, 88)], wo.at[pl.ds(88 * n, 88)]) for n in range(3)]
    pieces += [(ti, to), (hi, ho)]
    puts = [pltpu.make_async_copy(a, b, sem.at[i]) for i, (a, b) in enumerate(pieces)]
    for c in puts:
        c.start()
    for c in puts:
        c.wait()


def on_device(layer_input, head_input, out_grad, sensor_ids, valid_mask, sensor_table, proj_weight, step_bias, decay_log, skip_gain):
    pixels, dates, width = layer_input.shape
    total = pixels * dates * lax.axis_size("tile") * lax.axis_size("date")

    def heads(a):
        return a.reshape(pixels, dates, 8, 128).transpose(0, 2, 1, 3)

    any_ = pl.BlockSpec(memory_space=pl.ANY)
    vm = pl.BlockSpec(memory_space=pltpu.VMEM)
    four = (8, NT, 4, 128)

    def v(shape, dtype):
        return pltpu.VMEM(shape, dtype)

    sm = pltpu.SMEM
    scratch = [
        sm((4,), jnp.int32), v((4, NT), jnp.int32), v((2, 1024), F32), v((264, 1024), BF16), sm((8,), F32), sm((8,), F32), sm((8,), F32),
        v(four, BF16), v((LEN, 1024), BF16), v((128, 1024), BF16), v((LEN, 128), F32), v((3, NT, 4, 128), BF16),
        v((3, NT, 4, 128), BF16), v(four, BF16), v(four, BF16), v((LEN, 128), F32), v((8, LEN), F32), v((8, LEN), F32),
        v((LEN, LEN), F32), v((LEN, LEN), F32), v((8, LEN), F32), v((8, LEN), F32), v((8, 128), F32), v((128, LEN), F32),
        v(four, BF16), v((3, NT, 4, 128), BF16),
        v((3, NT, 4, 128), BF16), v((8, 128, 128), F32), v((8, 128, 128), BF16), v((8, 128, 128), BF16),
        v((8, 128, 128), BF16), v((8, 128, 128), BF16), v((128, 128), F32), v((8, 16, 128), BF16), v((8, 16, 128), BF16),
        v((16, 128), F32), v((8, 16, 128), F32), v((8, 16, 128), BF16), v((8, 8, 16, 128), BF16), v((8, 8, 16, 128), BF16),
        v((9, 8, 128), F32), v((9, 8, 128), F32), v((8, 2, 8, 128), F32), v((8, 2, 8, 128), F32), v((2, 8, 128), F32),
        v((8, 2, 8, 128), F32), v((2, 8, 128), F32), v((8, 2, 8, 128), F32), v((8, 128), F32), v((8, 8, 128), F32),
        pltpu.SemaphoreType.DMA((7,)), pltpu.SemaphoreType.DMA((8,)), pltpu.SemaphoreType.DMA((5,)), pltpu.SemaphoreType.DMA((18,)),
        pltpu.SemaphoreType.DMA((18,)), pltpu.SemaphoreType.DMA((8,)), pltpu.SemaphoreType.DMA((8,)),
    ]

    def kernel(*refs):
        body(1.0 / math.sqrt(total), *refs)

    vg, ig, wg, tg, hg = pl.pallas_call(
        kernel,
        name="mixer_backward",
        out_shape=(
            v((pixels, 8, dates, 128), BF16), v(four, BF16), v((264, 1024), F32),
            v((2, 1024), F32), v((3, 8), F32),
        ),
        in_specs=[any_] * 10,
        out_specs=(vm, vm, vm, vm, vm),
        scratch_shapes=scratch,
        compiler_params=pltpu.CompilerParams(collective_id=0, has_side_effects=True),
    )(
        heads(layer_input), heads(head_input), heads(out_grad), sensor_ids, valid_mask.T, sensor_table, proj_weight.T,
        step_bias, decay_log, skip_gain,
    )

    six = jax.ShapeDtypeStruct((pixels, 8, dates, 128), BF16)
    vg, ig, wg, tg, hg = pl.pallas_call(
        write_out,
        name="write_outputs",
        out_shape=(six, six, *(jax.ShapeDtypeStruct(a.shape, a.dtype) for a in (wg, tg, hg))),
        in_specs=[vm] * 5,
        out_specs=(any_,) * 5,
        scratch_shapes=[pltpu.SemaphoreType.DMA((17,))],
    )(*(pltpu.with_memory_space_constraint(a, pltpu.VMEM) for a in (vg, ig, wg, tg, hg)))

    def dates_first(a):
        return a.transpose(0, 2, 1, 3).reshape(pixels, dates, width)

    return dates_first(vg), dates_first(ig), wg.T, tg, hg


def solution(mesh):
    in_specs = (
        P("tile", "date", None), P("tile", "date", None), P("tile", "date", None), P("date"), P("tile", "date"),
        P(), P(), P(), P(), P(),
    )
    out_specs = (P("tile", "date", None), P("tile", "date", None), P(), P(), P())
    return jax.shard_map(on_device, mesh=mesh, in_specs=in_specs, out_specs=out_specs, check_vma=False)
```

```python
import math

import jax
import jax.numpy as jnp
from jax import lax
from jax.experimental import pallas as pl
from jax.experimental.pallas import tpu as pltpu
from jax.sharding import PartitionSpec as P

F32 = jnp.float32
BF16 = jnp.bfloat16
NEG_FILL = -1e30
NT = 64
RING = 8
EARLY = 6
OWN = 46
LEN = 256


def mm(a, b, dims):
    return lax.dot_general(a, b, (dims, ((), ())), preferred_element_type=F32)


def iota(shape, dim):
    return lax.broadcasted_iota(jnp.int32, shape, dim)


def body(
    scale,
    li, xh, yh, ids_h, valid_h, table_h, wt_h, bias_h, decay_h, skip_h,
    vg, ig, wg, tg, hg,
    ids, valid, table, wt, bias, decay, skip,
    libuf, mix, wdt, gate, psend,
    pair, xb, yb, l_s, lt_s, dtt_s, g_s, dg_s, r_s, p_s, sk_s, dd_s, vs, pgs,
    pgr, wfull, s0, r0, s1, r1, a1, s2, r2, s3, r3, q2, q1, p0,
    a0s, a0r, a1s, a1r, a2s, a2r, a3s, a3r, d4s, d4r,
    in_sem, lsem, own_sem, ss, rs, fs, fr,
):
    tile = lax.axis_index("tile")
    me = lax.axis_index("date")
    core = lax.rem(me, 2)
    cx = lax.rem(me // 2, RING)
    zh = me // (2 * RING)
    cy = lax.rem(tile, RING)
    zl = tile // RING
    cz = zh * 2 + zl
    fi = (1 - core) * cx + core * cy
    se = core * cx + (1 - core) * cy

    def at(x, y, z, c):
        return (lax.rem(z, 2) * RING + y, ((z // 2) * RING + x) * 2 + c)

    def first_peer(f):
        return at((1 - core) * f + core * cx, core * f + (1 - core) * cy, cz, core)

    def second_peer(s):
        return at(core * s + (1 - core) * cx, (1 - core) * s + core * cy, cz, core)

    def x_peer(x):
        return at(x, cy, cz, core)

    def y_peer(y):
        return at(cx, y, cz, core)

    def z_peer(z):
        return at(cx, cy, z, core)

    partner = at(cx, cy, cz, 1 - core)

    def offset(n):
        return ((n + 1) // 2) * (1 - 2 * lax.rem(n, 2))

    def chip(mine, u):
        return lax.rem(mine + RING // 2 + offset(u) + RING, RING)

    def ring(mine, step):
        def one(u, carry):
            step(chip(mine, u))
            return carry

        lax.fori_loop(0, RING - 1, one, 0)

    def near_ring(mine, step):
        def one(u, carry):
            step(chip(mine, RING - 2 - u))
            return carry

        lax.fori_loop(0, RING - 1, one, 0)

    def far_first(low, high, step):
        def one(k, carry):
            v = lax.rem(k // 2, 4)
            u = lax.rem(k // 8 + 2 * RING - 2 * v, RING)
            z = lax.rem(zh + 2 + offset(v) + 4, 4)
            x = chip(cx, u)
            step((z * RING + x) * 2 + lax.rem(core + k, 2))
            return carry

        for a, b in ((low, min(high, OWN)), (max(low, OWN + 1), high)):
            if a < b:
                lax.fori_loop(a, b, one, 0)

    def send(src, dst, i, to, recv=None):
        pltpu.make_async_remote_copy(
            src_ref=src, dst_ref=dst, send_sem=ss.at[i], recv_sem=rs.at[i] if recv is None else recv,
            device_id=to, device_id_type=pl.DeviceIdType.MESH,
        ).start()

    def drain(ref, sem):
        pltpu.make_async_copy(ref, ref, sem).wait()

    barrier = pltpu.get_barrier_semaphore()

    def greet(to):
        pl.semaphore_signal(barrier, inc=1, device_id=to, device_id_type=pl.DeviceIdType.MESH)

    far_first(0, NT, lambda d: greet((tile, d)))
    ring(cy, lambda y: greet(y_peer(y)))

    def greet_z(k, carry):
        greet(at(cx, cy, 2 * k + 1 - zl, core))
        return carry

    lax.fori_loop(0, RING // 2, greet_z, 0)

    smalls = [
        pltpu.make_async_copy(a, b, in_sem.at[i])
        for i, (a, b) in enumerate((
            (ids_h, ids), (valid_h, valid), (table_h, table), (wt_h, wt), (bias_h, bias), (decay_h, decay), (skip_h, skip),
        ))
    ]
    for c in smalls:
        c.start()
    loads = [pltpu.make_async_copy(li.at[:, k], libuf.at[k], lsem.at[k]) for k in range(8)]
    for c in loads:
        c.start()
    own_x = pltpu.make_async_copy(xh.at[me], xb.at[:, me], own_sem.at[0])
    own_y = pltpu.make_async_copy(yh.at[me], yb.at[:, me], own_sem.at[1])
    own_x.start()
    own_y.start()
    pl.semaphore_wait(barrier, (NT - 1) + (RING - 1) + RING // 2)
    far_first(0, NT, lambda d: send(yh.at[d], yb.at[:, me], 1, (tile, d)))

    for c in smalls:
        c.wait()
    row = iota((LEN, 128), 0)
    lane = iota((LEN, 128), 1)
    r3i = row & 3
    sens = jnp.where(r3i == 0, ids[0], jnp.where(r3i == 1, ids[1], jnp.where(r3i == 2, ids[2], ids[3])))
    is2 = sens == 1
    lif = libuf.reshape(8, LEN, 128)
    for k in range(8):
        loads[k].wait()
        cols = slice(128 * k, 128 * (k + 1))
        emb = jnp.where(is2, table[1:2, cols], table[0:1, cols])
        mix[:, cols] = (lif[k].astype(F32) + emb).astype(BF16)
    wdt[...] = jnp.zeros_like(wdt)
    wdt[0:8, :] = wt[256:264, :]
    pairs = mm(mix[...], wt[0:256, :], ((1,), (1,)))
    pre = mm(mix[...], wdt[...], ((1,), (1,)))
    lane1 = iota((1, 128), 1)
    bias_row = jnp.zeros((1, 128), F32)
    dec_row = jnp.zeros((1, 128), F32)
    for h in range(8):
        bias_row = jnp.where(lane1 == h, bias[h], bias_row)
        dec_row = jnp.where(lane1 == h, decay[h], dec_row)
    pre = pre + bias_row
    row6 = iota((LEN, NT), 0)
    col6 = iota((LEN, NT), 1)
    val = jnp.zeros((LEN, NT), F32)
    for t in range(4):
        val = jnp.where(((row6 >> 2) == col6) & ((row6 & 3) == t), valid[t : t + 1, :].astype(F32), val)
    val = jnp.sum(val, axis=1, keepdims=True)
    steps = jnp.where(lane < 8, val * jax.nn.softplus(pre), 0.0)
    gate[...] = jnp.where(lane < 8, val * jax.nn.sigmoid(pre), 0.0)
    psf = psend.reshape(3, LEN, 128)
    psf[0] = pairs[:, 0:128].astype(BF16)
    psf[1] = pairs[:, 128:256].astype(BF16)
    psf[2] = steps.astype(BF16)
    own_p = pltpu.make_async_copy(psend.at[:, me], pair.at[:, me], own_sem.at[2])
    own_p.start()

    far_first(0, NT, lambda d: send(psend.at[:, d], pair.at[:, me], 0, (tile, d)))
    far_first(0, NT, lambda d: send(xh.at[d, pl.ds(0, EARLY)], xb.at[pl.ds(0, EARLY), me], 2, (tile, d)))
    far_first(0, NT, lambda d: send(xh.at[d, pl.ds(EARLY, 8 - EARLY)], xb.at[pl.ds(EARLY, 8 - EARLY), me], 17, (tile, d)))

    i2 = iota((LEN, LEN), 0)
    j2 = iota((LEN, LEN), 1)
    a_row = -jnp.exp(dec_row)
    row8 = iota((8, 128), 0)
    lane8 = iota((8, 128), 1)
    a_col = jnp.sum(jnp.where(row8 == lane8, a_row, 0.0), axis=1, keepdims=True)
    tril = (i2 >= j2).astype(F32).astype(BF16)
    strict = (i2 < j2).astype(F32).astype(BF16)
    eye = (i2 == j2).astype(F32).astype(BF16)
    dg_s[...] = jnp.zeros_like(dg_s)
    dd_s[...] = jnp.zeros_like(dd_s)

    own_p.wait()
    drain(pair.at[:, pl.ds(0, NT - 1)], rs.at[0])
    pf = pair.reshape(3, LEN, 128)
    dtb = pf[2]
    l_s[...] = mm(tril, dtb, ((1,), (0,))) * a_row
    lt_s[...] = mm(dtb, tril, ((0,), (1,)))[0:8, :] * a_col
    dtt_s[...] = mm(dtb, eye, ((0,), (0,)))[0:8, :]
    g_s[...] = mm(pf[1], pf[0], ((1,), (1,)))

    own_x.wait()
    own_y.wait()
    drain(yb.at[:, pl.ds(0, NT - 1)], rs.at[1])
    drain(xb.at[pl.ds(0, EARLY), pl.ds(0, NT - 1)], rs.at[2])
    xf = xb.reshape(8, LEN, 128)
    yf = yb.reshape(8, LEN, 128)
    vf = vs.reshape(8, LEN, 128)

    def head(h, carry):
        pick = lane == h
        lc = jnp.sum(jnp.where(pick, l_s[...], 0.0), axis=1, keepdims=True)
        dtc = jnp.sum(jnp.where(pick, pf[2].astype(F32), 0.0), axis=1, keepdims=True)
        lr = lt_s[pl.ds(h, 1), :]
        dtr = dtt_s[pl.ds(h, 1), :]
        ker = jnp.exp(jnp.where(i2 >= j2, lc - lr, NEG_FILL))
        x = xf[h]
        y = yf[h]
        kz = ker * mm(y, x, ((1,), (1,)))
        dg_s[...] += kz * dtr
        g = g_s[...]
        both = kz * g
        p_s[pl.ds(h, 1), :] = jnp.sum(both, axis=0, keepdims=True)
        spread = mm((both * dtr).astype(BF16), strict, ((1,), (0,)))
        r_s[pl.ds(h, 1), :] = jnp.sum(jnp.where(i2 >= j2, spread, 0.0), axis=0, keepdims=True)
        dw = mm((ker * g).astype(BF16), y, ((0,), (0,)))
        y32 = y.astype(F32)
        vf[h] = (dw * dtc + skip[h] * y32).astype(BF16)
        sk_s[pl.ds(h, 1), :] = jnp.sum(y32 * x.astype(F32), axis=0, keepdims=True)
        return carry

    lax.fori_loop(0, EARLY, head, 0)
    drain(xb.at[pl.ds(EARLY, 8 - EARLY), pl.ds(0, NT - 1)], rs.at[17])
    lax.fori_loop(EARLY, 8, head, 0)
    pgf = pgs.reshape(3, LEN, 128)
    dgb = dg_s[...].astype(BF16)
    pgf[0] = mm(dgb, pf[1], ((0,), (0,))).astype(BF16)
    pgf[1] = mm(dgb, pf[0], ((1,), (0,))).astype(BF16)
    dd_s[0:8, :] = a_col * r_s[...] + p_s[...]
    pgf[2] = jnp.transpose(dd_s[...]).astype(BF16)
    own_g = pltpu.make_async_copy(pgs.at[:, me], pgr.at[:, me], own_sem.at[3])
    own_g.start()
    far_first(0, NT, lambda d: send(pgs.at[:, d], pgr.at[:, me], 3, (tile, d)))
    own_v = pltpu.make_async_copy(vs.at[:, me], vg.at[me], own_sem.at[4])
    own_v.start()

    def give_values(low, high):
        far_first(low, high, lambda d: send(vs.at[:, d], vg.at[me], 4, (tile, d)))

    give_values(0, 28)
    decay_col = a_col * jnp.sum(r_s[...] * dtt_s[...], axis=1, keepdims=True)
    skip_col = jnp.sum(sk_s[...], axis=1, keepdims=True)
    head_row = jnp.sum(
        jnp.where(lane8 == row8, decay_col, 0.0) + jnp.where(lane8 == row8 + 64, skip_col, 0.0), axis=0, keepdims=True
    )

    own_g.wait()
    drain(pgr.at[:, pl.ds(0, NT - 1)], rs.at[3])
    prf = pgr.reshape(3, LEN, 128)
    raw = prf[2].astype(F32) * gate[...]
    rawb = raw.astype(BF16)
    gb = prf[0]
    gc = prf[1]
    give = mm(prf[1 - core], mix[...], ((0,), (0,)))
    for k in range(8):
        s0[k] = give[:, 128 * k : 128 * (k + 1)].astype(BF16)
    send(s0, r0, 5, partner)
    keep = mm(prf[core], mix[...], ((0,), (0,)))
    for k in range(8):
        wfull[k] = keep[:, 128 * k : 128 * (k + 1)]
    wd = mm(rawb, mix[...], ((0,), (0,)))
    for k in range(8):
        a0s[k] = wd[0:8, 128 * k : 128 * (k + 1)]
    tok = iota((8, LEN), 1) & 3
    sens8 = jnp.where(tok == 0, ids[0], jnp.where(tok == 1, ids[1], jnp.where(tok == 2, ids[2], ids[3])))
    rows8 = iota((8, LEN), 0)
    sel = jnp.where(rows8 < 3, (sens8 != 1).astype(F32), jnp.where(rows8 < 6, (sens8 == 1).astype(F32), 0.0)).astype(BF16)
    sum_b = mm(sel, gb, ((1,), (0,)))
    sum_c = mm(sel, gc, ((1,), (0,)))
    sum_r = mm(sel, rawb, ((1,), (0,)))
    raw_sum = jnp.sum(raw, axis=0, keepdims=True)
    kind = jnp.where(row8 < 3, row8, row8 - 3)
    small = jnp.where(kind == 0, sum_b, jnp.where(kind == 1, sum_c, sum_r))
    small = jnp.where(row8 == 6, head_row, jnp.where(row8 == 7, raw_sum, small))
    a0s[8] = small
    send(a0s, a0r, 6, partner)

    drain(r0, rs.at[5])
    for k in range(8):
        both = wfull[k] + r0[k].astype(F32)
        wfull[k] = both
        s1[k] = both.astype(BF16)
    ring(fi, lambda f: send(s1.at[f], r1.at[fi], 7, first_peer(f)))
    drain(a0r, rs.at[6])
    for k in range(8):
        a1s[k, 0] = a0s[k] + a0r[k]
        a1s[k, 1] = a0s[8] + a0r[8]
    a1r[cz] = a1s[cz]
    ring(cz, lambda z: send(a1s.at[z], a1r.at[cz], 8, z_peer(z)))

    igf = ig.reshape(8, LEN, 128)

    def input_grad(low, high):
        for k in range(low, high):
            cols = slice(128 * k, 128 * (k + 1))
            flat = mm(gb, wt[0:128, cols], ((1,), (0,))) + mm(gc, wt[128:256, cols], ((1,), (0,)))
            igf[k] = (flat + mm(rawb, wdt[:, cols], ((1,), (0,)))).astype(BF16)

    input_grad(0, 2)

    drain(r1.at[pl.ds(0, RING - 1)], rs.at[7])
    a1[...] = wfull[fi]

    def add1(k, carry):
        a1[...] += r1[lax.rem(fi + k, RING)].astype(F32)
        return carry

    lax.fori_loop(1, RING, add1, 0)
    s2[...] = a1[...].astype(BF16).reshape(RING, 16, 128)
    ring(se, lambda s: send(s2.at[s], r2.at[se], 9, second_peer(s)))
    drain(a1r.at[pl.ds(0, RING - 1)], rs.at[8])
    a2s[...] = ((a1r[0] + a1r[1]) + (a1r[2] + a1r[3])) + ((a1r[4] + a1r[5]) + (a1r[6] + a1r[7]))
    a2r[cy] = a2s[...]
    ring(cy, lambda y: send(a2s, a2r.at[cy], 10, y_peer(y)))
    give_values(28, 40)
    input_grad(2, 4)

    drain(r2.at[pl.ds(0, RING - 1)], rs.at[9])
    s3[...] = a1[pl.ds(pl.multiple_of(se * 16, 16), 16), :]

    def add2(k, carry):
        s3[...] += r2[lax.rem(se + k, RING)].astype(F32)
        return carry

    lax.fori_loop(1, RING, add2, 0)
    r3[cz] = s3[...]
    ring(cz, lambda z: send(s3, r3.at[cz], 11, z_peer(z)))
    drain(a2r.at[pl.ds(0, RING - 1)], rs.at[10])
    a3s[...] = ((a2r[0] + a2r[1]) + (a2r[2] + a2r[3])) + ((a2r[4] + a2r[5]) + (a2r[6] + a2r[7]))
    a3r[cx] = a3s[...]
    ring(cx, lambda x: send(a3s, a3r.at[cx], 12, x_peer(x)))
    give_values(40, 52)
    input_grad(4, 6)

    drain(r3.at[pl.ds(0, RING - 1)], rs.at[11])
    total = ((r3[0] + r3[1]) + (r3[2] + r3[3])) + ((r3[4] + r3[5]) + (r3[6] + r3[7]))
    q2[se] = (total * scale).astype(BF16)
    ring(se, lambda s: send(q2.at[se], q2.at[se], 13, second_peer(s)))
    drain(a3r.at[pl.ds(0, RING - 1)], rs.at[12])
    aux = ((a3r[0] + a3r[1]) + (a3r[2] + a3r[3])) + ((a3r[4] + a3r[5]) + (a3r[6] + a3r[7]))
    aux = aux * scale
    d4s[...] = aux[0]
    d4r[cz] = aux[0]
    ring(cz, lambda z: send(d4s, d4r.at[cz], 14, z_peer(z)))
    give_values(52, NT)
    input_grad(6, 8)
    small = aux[1]

    drain(q2.at[pl.ds(0, RING - 1)], rs.at[13])
    send(q2, p0.at[fi], 15, partner, fr.at[fi])
    ring(fi, lambda f: send(q2, q1.at[fi], 16, first_peer(f), fs.at[fi]))
    q1[fi] = q2[...]

    hi = small.astype(BF16)
    left = small - hi.astype(F32)
    mid = left.astype(BF16)
    low = (left - mid.astype(F32)).astype(BF16)

    def times(w):
        return mm(hi, w, ((1,), (0,))) + (mm(mid, w, ((1,), (0,))) + mm(low, w, ((1,), (0,))))

    tb = times(wt[0:128, :])
    tc = times(wt[128:256, :])
    tr = times(wdt[...])
    tg[0:1, :] = tb[0:1] + tc[1:2] + tr[2:3]
    tg[1:2, :] = tb[3:4] + tc[4:5] + tr[5:6]
    hg[0:1, :] = small[6:7, 0:8]
    hg[1:2, :] = small[7:8, 0:8]
    hg[2:3, :] = pltpu.roll(small, 64, 1)[6:7, 0:8]
    drain(d4r.at[pl.ds(0, RING - 1)], rs.at[14])
    for k in range(8):
        wg[256:264, 128 * k : 128 * (k + 1)] = d4r[k]

    mine = pl.multiple_of(core * 128, 128)
    other = pl.multiple_of((1 - core) * 128, 128)

    def keep_piece(first, f, piece):
        wg[pl.ds(first, 128), pl.ds(pl.multiple_of(f * 128, 128), 128)] = piece[f].reshape(128, 128).astype(F32)

    def pass_on(f):
        drain(q1.at[f], fs.at[f])
        send(q1.at[f], p0.at[f], 15, partner, fr.at[f])
        keep_piece(mine, f, q1)

    def take(f):
        drain(p0.at[f], fr.at[f])
        keep_piece(other, f, p0)

    keep_piece(mine, fi, q1)
    near_ring(fi, pass_on)
    partner_fi = (1 - core) * cy + core * cx
    take(partner_fi)
    near_ring(partner_fi, take)

    own_v.wait()
    drain(vs.at[:, pl.ds(0, NT - 1)], rs.at[4])
    drain(psend.at[:, pl.ds(0, NT - 1)], ss.at[0])
    drain(yb.at[:, pl.ds(0, NT - 1)], ss.at[1])
    drain(xb.at[pl.ds(0, EARLY), pl.ds(0, NT - 1)], ss.at[2])
    drain(xb.at[pl.ds(EARLY, 8 - EARLY), pl.ds(0, NT - 1)], ss.at[17])
    drain(pgs.at[:, pl.ds(0, NT - 1)], ss.at[3])
    drain(vs.at[:, pl.ds(0, NT - 1)], ss.at[4])
    drain(s0, ss.at[5])
    drain(a0s, ss.at[6])
    drain(s1.at[pl.ds(0, RING - 1)], ss.at[7])
    drain(a1s.at[pl.ds(0, RING - 1)], ss.at[8])
    drain(s2.at[pl.ds(0, RING - 1)], ss.at[9])
    drain(a2r.at[pl.ds(0, RING - 1)], ss.at[10])
    drain(r3.at[pl.ds(0, RING - 1)], ss.at[11])
    drain(a3r.at[pl.ds(0, RING - 1)], ss.at[12])
    drain(q2.at[pl.ds(0, RING - 1)], ss.at[13])
    drain(d4r.at[pl.ds(0, RING - 1)], ss.at[14])
    drain(p0, ss.at[15])
    drain(q1.at[pl.ds(0, RING - 1)], ss.at[16])


def write_out(vi, ii, wi, ti, hi, vo, io, wo, to, ho, sem):
    pieces = [(vi.at[pl.ds(16 * n, 16)], vo.at[pl.ds(16 * n, 16)]) for n in range(4)]
    pieces += [(ii.at[k], io.at[:, k]) for k in range(8)]
    pieces += [(wi.at[pl.ds(88 * n, 88)], wo.at[pl.ds(88 * n, 88)]) for n in range(3)]
    pieces += [(ti, to), (hi, ho)]
    puts = [pltpu.make_async_copy(a, b, sem.at[i]) for i, (a, b) in enumerate(pieces)]
    for c in puts:
        c.start()
    for c in puts:
        c.wait()


def on_device(layer_input, head_input, out_grad, sensor_ids, valid_mask, sensor_table, proj_weight, step_bias, decay_log, skip_gain):
    pixels, dates, width = layer_input.shape
    total = pixels * dates * lax.axis_size("tile") * lax.axis_size("date")

    def heads(a):
        return a.reshape(pixels, dates, 8, 128).transpose(0, 2, 1, 3)

    any_ = pl.BlockSpec(memory_space=pl.ANY)
    vm = pl.BlockSpec(memory_space=pltpu.VMEM)
    four = (8, NT, 4, 128)

    def v(shape, dtype):
        return pltpu.VMEM(shape, dtype)

    sm = pltpu.SMEM
    scratch = [
        sm((4,), jnp.int32), v((4, NT), jnp.int32), v((2, 1024), F32), v((264, 1024), BF16), sm((8,), F32), sm((8,), F32), sm((8,), F32),
        v(four, BF16), v((LEN, 1024), BF16), v((128, 1024), BF16), v((LEN, 128), F32), v((3, NT, 4, 128), BF16),
        v((3, NT, 4, 128), BF16), v(four, BF16), v(four, BF16), v((LEN, 128), F32), v((8, LEN), F32), v((8, LEN), F32),
        v((LEN, LEN), F32), v((LEN, LEN), F32), v((8, LEN), F32), v((8, LEN), F32), v((8, 128), F32), v((128, LEN), F32),
        v(four, BF16), v((3, NT, 4, 128), BF16),
        v((3, NT, 4, 128), BF16), v((8, 128, 128), F32), v((8, 128, 128), BF16), v((8, 128, 128), BF16),
        v((8, 128, 128), BF16), v((8, 128, 128), BF16), v((128, 128), F32), v((8, 16, 128), BF16), v((8, 16, 128), BF16),
        v((16, 128), F32), v((8, 16, 128), F32), v((8, 16, 128), BF16), v((8, 8, 16, 128), BF16), v((8, 8, 16, 128), BF16),
        v((9, 8, 128), F32), v((9, 8, 128), F32), v((8, 2, 8, 128), F32), v((8, 2, 8, 128), F32), v((2, 8, 128), F32),
        v((8, 2, 8, 128), F32), v((2, 8, 128), F32), v((8, 2, 8, 128), F32), v((8, 128), F32), v((8, 8, 128), F32),
        pltpu.SemaphoreType.DMA((7,)), pltpu.SemaphoreType.DMA((8,)), pltpu.SemaphoreType.DMA((5,)), pltpu.SemaphoreType.DMA((18,)),
        pltpu.SemaphoreType.DMA((18,)), pltpu.SemaphoreType.DMA((8,)), pltpu.SemaphoreType.DMA((8,)),
    ]

    def kernel(*refs):
        body(1.0 / math.sqrt(total), *refs)

    vg, ig, wg, tg, hg = pl.pallas_call(
        kernel,
        name="mixer_backward",
        out_shape=(
            v((pixels, 8, dates, 128), BF16), v(four, BF16), v((264, 1024), F32),
            v((2, 1024), F32), v((3, 8), F32),
        ),
        in_specs=[any_] * 10,
        out_specs=(vm, vm, vm, vm, vm),
        scratch_shapes=scratch,
        compiler_params=pltpu.CompilerParams(collective_id=0, has_side_effects=True),
    )(
        heads(layer_input), heads(head_input), heads(out_grad), sensor_ids, valid_mask.T, sensor_table, proj_weight.T,
        step_bias, decay_log, skip_gain,
    )

    six = jax.ShapeDtypeStruct((pixels, 8, dates, 128), BF16)
    vg, ig, wg, tg, hg = pl.pallas_call(
        write_out,
        name="write_outputs",
        out_shape=(six, six, *(jax.ShapeDtypeStruct(a.shape, a.dtype) for a in (wg, tg, hg))),
        in_specs=[vm] * 5,
        out_specs=(any_,) * 5,
        scratch_shapes=[pltpu.SemaphoreType.DMA((17,))],
    )(*(pltpu.with_memory_space_constraint(a, pltpu.VMEM) for a in (vg, ig, wg, tg, hg)))

    def dates_first(a):
        return a.transpose(0, 2, 1, 3).reshape(pixels, dates, width)

    return dates_first(vg), dates_first(ig), wg.T, tg, hg


def solution(mesh):
    in_specs = (
        P("tile", "date", None), P("tile", "date", None), P("tile", "date", None), P("date"), P("tile", "date"),
        P(), P(), P(), P(), P(),
    )
    out_specs = (P("tile", "date", None), P("tile", "date", None), P(), P(), P())
    return jax.shard_map(on_device, mesh=mesh, in_specs=in_specs, out_specs=out_specs, check_vma=False)
```

```python
import math

import jax
import jax.numpy as jnp
from jax import lax
from jax.experimental import pallas as pl
from jax.experimental.pallas import tpu as pltpu
from jax.sharding import PartitionSpec as P

F32 = jnp.float32
BF16 = jnp.bfloat16
NEG_FILL = -1e30
NT = 64
RING = 8
EARLY = 7
OWN = 46
LEN = 256


def mm(a, b, dims):
    return lax.dot_general(a, b, (dims, ((), ())), preferred_element_type=F32)


def iota(shape, dim):
    return lax.broadcasted_iota(jnp.int32, shape, dim)


def body(
    scale,
    li, xh, yh, ids_h, valid_h, table_h, wt_h, bias_h, decay_h, skip_h,
    vg, ig, wg, tg, hg,
    ids, valid, table, wt, bias, decay, skip,
    libuf, mix, wdt, gate, psend,
    pair, xb, yb, l_s, lt_s, dtt_s, g_s, dg_s, r_s, p_s, sk_s, dd_s, vs, pgs,
    pgr, wfull, s0, r0, s1, r1, a1, s2, r2, s3, r3, q2, q1, p0,
    a0s, a0r, a1s, a1r, a2s, a2r, a3s, a3r, d4s, d4r,
    in_sem, lsem, own_sem, ss, rs, fs, fr,
):
    tile = lax.axis_index("tile")
    me = lax.axis_index("date")
    core = lax.rem(me, 2)
    cx = lax.rem(me // 2, RING)
    zh = me // (2 * RING)
    cy = lax.rem(tile, RING)
    zl = tile // RING
    cz = zh * 2 + zl
    fi = (1 - core) * cx + core * cy
    se = core * cx + (1 - core) * cy

    def at(x, y, z, c):
        return (lax.rem(z, 2) * RING + y, ((z // 2) * RING + x) * 2 + c)

    def first_peer(f):
        return at((1 - core) * f + core * cx, core * f + (1 - core) * cy, cz, core)

    def second_peer(s):
        return at(core * s + (1 - core) * cx, (1 - core) * s + core * cy, cz, core)

    def x_peer(x):
        return at(x, cy, cz, core)

    def y_peer(y):
        return at(cx, y, cz, core)

    def z_peer(z):
        return at(cx, cy, z, core)

    partner = at(cx, cy, cz, 1 - core)

    def offset(n):
        return ((n + 1) // 2) * (1 - 2 * lax.rem(n, 2))

    def chip(mine, u):
        return lax.rem(mine + RING // 2 + offset(u) + RING, RING)

    def ring(mine, step):
        def one(u, carry):
            step(chip(mine, u))
            return carry

        lax.fori_loop(0, RING - 1, one, 0)

    def near_ring(mine, step):
        def one(u, carry):
            step(chip(mine, RING - 2 - u))
            return carry

        lax.fori_loop(0, RING - 1, one, 0)

    def far_first(low, high, step):
        def one(k, carry):
            v = lax.rem(k // 2, 4)
            u = lax.rem(k // 8 + 2 * RING - 2 * v, RING)
            z = lax.rem(zh + 2 + offset(v) + 4, 4)
            x = chip(cx, u)
            step((z * RING + x) * 2 + lax.rem(core + k, 2))
            return carry

        for a, b in ((low, min(high, OWN)), (max(low, OWN + 1), high)):
            if a < b:
                lax.fori_loop(a, b, one, 0)

    def send(src, dst, i, to, recv=None):
        pltpu.make_async_remote_copy(
            src_ref=src, dst_ref=dst, send_sem=ss.at[i], recv_sem=rs.at[i] if recv is None else recv,
            device_id=to, device_id_type=pl.DeviceIdType.MESH,
        ).start()

    def drain(ref, sem):
        pltpu.make_async_copy(ref, ref, sem).wait()

    barrier = pltpu.get_barrier_semaphore()

    def greet(to):
        pl.semaphore_signal(barrier, inc=1, device_id=to, device_id_type=pl.DeviceIdType.MESH)

    far_first(0, NT, lambda d: greet((tile, d)))
    ring(cy, lambda y: greet(y_peer(y)))

    def greet_z(k, carry):
        greet(at(cx, cy, 2 * k + 1 - zl, core))
        return carry

    lax.fori_loop(0, RING // 2, greet_z, 0)

    smalls = [
        pltpu.make_async_copy(a, b, in_sem.at[i])
        for i, (a, b) in enumerate((
            (ids_h, ids), (valid_h, valid), (table_h, table), (wt_h, wt), (bias_h, bias), (decay_h, decay), (skip_h, skip),
        ))
    ]
    for c in smalls:
        c.start()
    loads = [pltpu.make_async_copy(li.at[:, k], libuf.at[k], lsem.at[k]) for k in range(8)]
    for c in loads:
        c.start()
    own_x = pltpu.make_async_copy(xh.at[me], xb.at[:, me], own_sem.at[0])
    own_y = pltpu.make_async_copy(yh.at[me], yb.at[:, me], own_sem.at[1])
    own_x.start()
    own_y.start()
    pl.semaphore_wait(barrier, (NT - 1) + (RING - 1) + RING // 2)
    far_first(0, NT, lambda d: send(yh.at[d], yb.at[:, me], 1, (tile, d)))

    for c in smalls:
        c.wait()
    row = iota((LEN, 128), 0)
    lane = iota((LEN, 128), 1)
    r3i = row & 3
    sens = jnp.where(r3i == 0, ids[0], jnp.where(r3i == 1, ids[1], jnp.where(r3i == 2, ids[2], ids[3])))
    is2 = sens == 1
    lif = libuf.reshape(8, LEN, 128)
    for k in range(8):
        loads[k].wait()
        cols = slice(128 * k, 128 * (k + 1))
        emb = jnp.where(is2, table[1:2, cols], table[0:1, cols])
        mix[:, cols] = (lif[k].astype(F32) + emb).astype(BF16)
    wdt[...] = jnp.zeros_like(wdt)
    wdt[0:8, :] = wt[256:264, :]
    pairs = mm(mix[...], wt[0:256, :], ((1,), (1,)))
    pre = mm(mix[...], wdt[...], ((1,), (1,)))
    lane1 = iota((1, 128), 1)
    bias_row = jnp.zeros((1, 128), F32)
    dec_row = jnp.zeros((1, 128), F32)
    for h in range(8):
        bias_row = jnp.where(lane1 == h, bias[h], bias_row)
        dec_row = jnp.where(lane1 == h, decay[h], dec_row)
    pre = pre + bias_row
    row6 = iota((LEN, NT), 0)
    col6 = iota((LEN, NT), 1)
    val = jnp.zeros((LEN, NT), F32)
    for t in range(4):
        val = jnp.where(((row6 >> 2) == col6) & ((row6 & 3) == t), valid[t : t + 1, :].astype(F32), val)
    val = jnp.sum(val, axis=1, keepdims=True)
    steps = jnp.where(lane < 8, val * jax.nn.softplus(pre), 0.0)
    gate[...] = jnp.where(lane < 8, val * jax.nn.sigmoid(pre), 0.0)
    psf = psend.reshape(3, LEN, 128)
    psf[0] = pairs[:, 0:128].astype(BF16)
    psf[1] = pairs[:, 128:256].astype(BF16)
    psf[2] = steps.astype(BF16)
    own_p = pltpu.make_async_copy(psend.at[:, me], pair.at[:, me], own_sem.at[2])
    own_p.start()

    far_first(0, NT, lambda d: send(psend.at[:, d], pair.at[:, me], 0, (tile, d)))
    far_first(0, NT, lambda d: send(xh.at[d, pl.ds(0, EARLY)], xb.at[pl.ds(0, EARLY), me], 2, (tile, d)))
    far_first(0, NT, lambda d: send(xh.at[d, pl.ds(EARLY, 8 - EARLY)], xb.at[pl.ds(EARLY, 8 - EARLY), me], 17, (tile, d)))

    i2 = iota((LEN, LEN), 0)
    j2 = iota((LEN, LEN), 1)
    a_row = -jnp.exp(dec_row)
    row8 = iota((8, 128), 0)
    lane8 = iota((8, 128), 1)
    a_col = jnp.sum(jnp.where(row8 == lane8, a_row, 0.0), axis=1, keepdims=True)
    tril = (i2 >= j2).astype(F32).astype(BF16)
    strict = (i2 < j2).astype(F32).astype(BF16)
    eye = (i2 == j2).astype(F32).astype(BF16)
    dg_s[...] = jnp.zeros_like(dg_s)
    dd_s[...] = jnp.zeros_like(dd_s)

    own_p.wait()
    drain(pair.at[:, pl.ds(0, NT - 1)], rs.at[0])
    pf = pair.reshape(3, LEN, 128)
    dtb = pf[2]
    l_s[...] = mm(tril, dtb, ((1,), (0,))) * a_row
    lt_s[...] = mm(dtb, tril, ((0,), (1,)))[0:8, :] * a_col
    dtt_s[...] = mm(dtb, eye, ((0,), (0,)))[0:8, :]
    g_s[...] = mm(pf[1], pf[0], ((1,), (1,)))

    own_x.wait()
    own_y.wait()
    drain(yb.at[:, pl.ds(0, NT - 1)], rs.at[1])
    drain(xb.at[pl.ds(0, EARLY), pl.ds(0, NT - 1)], rs.at[2])
    xf = xb.reshape(8, LEN, 128)
    yf = yb.reshape(8, LEN, 128)
    vf = vs.reshape(8, LEN, 128)

    def head(h, carry):
        pick = lane == h
        lc = jnp.sum(jnp.where(pick, l_s[...], 0.0), axis=1, keepdims=True)
        dtc = jnp.sum(jnp.where(pick, pf[2].astype(F32), 0.0), axis=1, keepdims=True)
        lr = lt_s[pl.ds(h, 1), :]
        dtr = dtt_s[pl.ds(h, 1), :]
        ker = jnp.exp(jnp.where(i2 >= j2, lc - lr, NEG_FILL))
        x = xf[h]
        y = yf[h]
        kz = ker * mm(y, x, ((1,), (1,)))
        dg_s[...] += kz * dtr
        g = g_s[...]
        both = kz * g
        p_s[pl.ds(h, 1), :] = jnp.sum(both, axis=0, keepdims=True)
        spread = mm((both * dtr).astype(BF16), strict, ((1,), (0,)))
        r_s[pl.ds(h, 1), :] = jnp.sum(jnp.where(i2 >= j2, spread, 0.0), axis=0, keepdims=True)
        dw = mm((ker * g).astype(BF16), y, ((0,), (0,)))
        y32 = y.astype(F32)
        vf[h] = (dw * dtc + skip[h] * y32).astype(BF16)
        sk_s[pl.ds(h, 1), :] = jnp.sum(y32 * x.astype(F32), axis=0, keepdims=True)
        return carry

    lax.fori_loop(0, EARLY, head, 0)
    drain(xb.at[pl.ds(EARLY, 8 - EARLY), pl.ds(0, NT - 1)], rs.at[17])
    lax.fori_loop(EARLY, 8, head, 0)
    pgf = pgs.reshape(3, LEN, 128)
    dgb = dg_s[...].astype(BF16)
    pgf[0] = mm(dgb, pf[1], ((0,), (0,))).astype(BF16)
    pgf[1] = mm(dgb, pf[0], ((1,), (0,))).astype(BF16)
    dd_s[0:8, :] = a_col * r_s[...] + p_s[...]
    pgf[2] = jnp.transpose(dd_s[...]).astype(BF16)
    own_g = pltpu.make_async_copy(pgs.at[:, me], pgr.at[:, me], own_sem.at[3])
    own_g.start()
    far_first(0, NT, lambda d: send(pgs.at[:, d], pgr.at[:, me], 3, (tile, d)))
    own_v = pltpu.make_async_copy(vs.at[:, me], vg.at[me], own_sem.at[4])
    own_v.start()

    def give_values(low, high):
        far_first(low, high, lambda d: send(vs.at[:, d], vg.at[me], 4, (tile, d)))

    give_values(0, 28)
    decay_col = a_col * jnp.sum(r_s[...] * dtt_s[...], axis=1, keepdims=True)
    skip_col = jnp.sum(sk_s[...], axis=1, keepdims=True)
    head_row = jnp.sum(
        jnp.where(lane8 == row8, decay_col, 0.0) + jnp.where(lane8 == row8 + 64, skip_col, 0.0), axis=0, keepdims=True
    )

    own_g.wait()
    drain(pgr.at[:, pl.ds(0, NT - 1)], rs.at[3])
    prf = pgr.reshape(3, LEN, 128)
    raw = prf[2].astype(F32) * gate[...]
    rawb = raw.astype(BF16)
    gb = prf[0]
    gc = prf[1]
    give = mm(prf[1 - core], mix[...], ((0,), (0,)))
    for k in range(8):
        s0[k] = give[:, 128 * k : 128 * (k + 1)].astype(BF16)
    send(s0, r0, 5, partner)
    keep = mm(prf[core], mix[...], ((0,), (0,)))
    for k in range(8):
        wfull[k] = keep[:, 128 * k : 128 * (k + 1)]
    wd = mm(rawb, mix[...], ((0,), (0,)))
    for k in range(8):
        a0s[k] = wd[0:8, 128 * k : 128 * (k + 1)]
    tok = iota((8, LEN), 1) & 3
    sens8 = jnp.where(tok == 0, ids[0], jnp.where(tok == 1, ids[1], jnp.where(tok == 2, ids[2], ids[3])))
    rows8 = iota((8, LEN), 0)
    sel = jnp.where(rows8 < 3, (sens8 != 1).astype(F32), jnp.where(rows8 < 6, (sens8 == 1).astype(F32), 0.0)).astype(BF16)
    sum_b = mm(sel, gb, ((1,), (0,)))
    sum_c = mm(sel, gc, ((1,), (0,)))
    sum_r = mm(sel, rawb, ((1,), (0,)))
    raw_sum = jnp.sum(raw, axis=0, keepdims=True)
    kind = jnp.where(row8 < 3, row8, row8 - 3)
    small = jnp.where(kind == 0, sum_b, jnp.where(kind == 1, sum_c, sum_r))
    small = jnp.where(row8 == 6, head_row, jnp.where(row8 == 7, raw_sum, small))
    a0s[8] = small
    send(a0s, a0r, 6, partner)

    drain(r0, rs.at[5])
    for k in range(8):
        both = wfull[k] + r0[k].astype(F32)
        wfull[k] = both
        s1[k] = both.astype(BF16)
    ring(fi, lambda f: send(s1.at[f], r1.at[fi], 7, first_peer(f)))
    drain(a0r, rs.at[6])
    for k in range(8):
        a1s[k, 0] = a0s[k] + a0r[k]
        a1s[k, 1] = a0s[8] + a0r[8]
    a1r[cz] = a1s[cz]
    ring(cz, lambda z: send(a1s.at[z], a1r.at[cz], 8, z_peer(z)))

    igf = ig.reshape(8, LEN, 128)

    def input_grad(low, high):
        for k in range(low, high):
            cols = slice(128 * k, 128 * (k + 1))
            flat = mm(gb, wt[0:128, cols], ((1,), (0,))) + mm(gc, wt[128:256, cols], ((1,), (0,)))
            igf[k] = (flat + mm(rawb, wdt[:, cols], ((1,), (0,)))).astype(BF16)

    input_grad(0, 2)

    drain(r1.at[pl.ds(0, RING - 1)], rs.at[7])
    a1[...] = wfull[fi]

    def add1(k, carry):
        a1[...] += r1[lax.rem(fi + k, RING)].astype(F32)
        return carry

    lax.fori_loop(1, RING, add1, 0)
    s2[...] = a1[...].astype(BF16).reshape(RING, 16, 128)
    ring(se, lambda s: send(s2.at[s], r2.at[se], 9, second_peer(s)))
    drain(a1r.at[pl.ds(0, RING - 1)], rs.at[8])
    a2s[...] = ((a1r[0] + a1r[1]) + (a1r[2] + a1r[3])) + ((a1r[4] + a1r[5]) + (a1r[6] + a1r[7]))
    a2r[cy] = a2s[...]
    ring(cy, lambda y: send(a2s, a2r.at[cy], 10, y_peer(y)))
    give_values(28, 40)
    input_grad(2, 4)

    drain(r2.at[pl.ds(0, RING - 1)], rs.at[9])
    s3[...] = a1[pl.ds(pl.multiple_of(se * 16, 16), 16), :]

    def add2(k, carry):
        s3[...] += r2[lax.rem(se + k, RING)].astype(F32)
        return carry

    lax.fori_loop(1, RING, add2, 0)
    r3[cz] = s3[...]
    ring(cz, lambda z: send(s3, r3.at[cz], 11, z_peer(z)))
    drain(a2r.at[pl.ds(0, RING - 1)], rs.at[10])
    a3s[...] = ((a2r[0] + a2r[1]) + (a2r[2] + a2r[3])) + ((a2r[4] + a2r[5]) + (a2r[6] + a2r[7]))
    a3r[cx] = a3s[...]
    ring(cx, lambda x: send(a3s, a3r.at[cx], 12, x_peer(x)))
    give_values(40, 52)
    input_grad(4, 6)

    drain(r3.at[pl.ds(0, RING - 1)], rs.at[11])
    total = ((r3[0] + r3[1]) + (r3[2] + r3[3])) + ((r3[4] + r3[5]) + (r3[6] + r3[7]))
    q2[se] = (total * scale).astype(BF16)
    ring(se, lambda s: send(q2.at[se], q2.at[se], 13, second_peer(s)))
    drain(a3r.at[pl.ds(0, RING - 1)], rs.at[12])
    aux = ((a3r[0] + a3r[1]) + (a3r[2] + a3r[3])) + ((a3r[4] + a3r[5]) + (a3r[6] + a3r[7]))
    aux = aux * scale
    d4s[...] = aux[0]
    d4r[cz] = aux[0]
    ring(cz, lambda z: send(d4s, d4r.at[cz], 14, z_peer(z)))
    give_values(52, NT)
    input_grad(6, 8)
    small = aux[1]

    drain(q2.at[pl.ds(0, RING - 1)], rs.at[13])
    send(q2, p0.at[fi], 15, partner, fr.at[fi])
    ring(fi, lambda f: send(q2, q1.at[fi], 16, first_peer(f), fs.at[fi]))
    q1[fi] = q2[...]

    hi = small.astype(BF16)
    left = small - hi.astype(F32)
    mid = left.astype(BF16)
    low = (left - mid.astype(F32)).astype(BF16)

    def times(w):
        return mm(hi, w, ((1,), (0,))) + (mm(mid, w, ((1,), (0,))) + mm(low, w, ((1,), (0,))))

    tb = times(wt[0:128, :])
    tc = times(wt[128:256, :])
    tr = times(wdt[...])
    tg[0:1, :] = tb[0:1] + tc[1:2] + tr[2:3]
    tg[1:2, :] = tb[3:4] + tc[4:5] + tr[5:6]
    hg[0:1, :] = small[6:7, 0:8]
    hg[1:2, :] = small[7:8, 0:8]
    hg[2:3, :] = pltpu.roll(small, 64, 1)[6:7, 0:8]
    drain(d4r.at[pl.ds(0, RING - 1)], rs.at[14])
    for k in range(8):
        wg[256:264, 128 * k : 128 * (k + 1)] = d4r[k]

    mine = pl.multiple_of(core * 128, 128)
    other = pl.multiple_of((1 - core) * 128, 128)

    def keep_piece(first, f, piece):
        wg[pl.ds(first, 128), pl.ds(pl.multiple_of(f * 128, 128), 128)] = piece[f].reshape(128, 128).astype(F32)

    def pass_on(f):
        drain(q1.at[f], fs.at[f])
        send(q1.at[f], p0.at[f], 15, partner, fr.at[f])
        keep_piece(mine, f, q1)

    def take(f):
        drain(p0.at[f], fr.at[f])
        keep_piece(other, f, p0)

    keep_piece(mine, fi, q1)
    near_ring(fi, pass_on)
    partner_fi = (1 - core) * cy + core * cx
    take(partner_fi)
    near_ring(partner_fi, take)

    own_v.wait()
    drain(vs.at[:, pl.ds(0, NT - 1)], rs.at[4])
    drain(psend.at[:, pl.ds(0, NT - 1)], ss.at[0])
    drain(yb.at[:, pl.ds(0, NT - 1)], ss.at[1])
    drain(xb.at[pl.ds(0, EARLY), pl.ds(0, NT - 1)], ss.at[2])
    drain(xb.at[pl.ds(EARLY, 8 - EARLY), pl.ds(0, NT - 1)], ss.at[17])
    drain(pgs.at[:, pl.ds(0, NT - 1)], ss.at[3])
    drain(vs.at[:, pl.ds(0, NT - 1)], ss.at[4])
    drain(s0, ss.at[5])
    drain(a0s, ss.at[6])
    drain(s1.at[pl.ds(0, RING - 1)], ss.at[7])
    drain(a1s.at[pl.ds(0, RING - 1)], ss.at[8])
    drain(s2.at[pl.ds(0, RING - 1)], ss.at[9])
    drain(a2r.at[pl.ds(0, RING - 1)], ss.at[10])
    drain(r3.at[pl.ds(0, RING - 1)], ss.at[11])
    drain(a3r.at[pl.ds(0, RING - 1)], ss.at[12])
    drain(q2.at[pl.ds(0, RING - 1)], ss.at[13])
    drain(d4r.at[pl.ds(0, RING - 1)], ss.at[14])
    drain(p0, ss.at[15])
    drain(q1.at[pl.ds(0, RING - 1)], ss.at[16])


def write_out(vi, ii, wi, ti, hi, vo, io, wo, to, ho, sem):
    pieces = [(vi.at[pl.ds(16 * n, 16)], vo.at[pl.ds(16 * n, 16)]) for n in range(4)]
    pieces += [(ii.at[k], io.at[:, k]) for k in range(8)]
    pieces += [(wi.at[pl.ds(88 * n, 88)], wo.at[pl.ds(88 * n, 88)]) for n in range(3)]
    pieces += [(ti, to), (hi, ho)]
    puts = [pltpu.make_async_copy(a, b, sem.at[i]) for i, (a, b) in enumerate(pieces)]
    for c in puts:
        c.start()
    for c in puts:
        c.wait()


def on_device(layer_input, head_input, out_grad, sensor_ids, valid_mask, sensor_table, proj_weight, step_bias, decay_log, skip_gain):
    pixels, dates, width = layer_input.shape
    total = pixels * dates * lax.axis_size("tile") * lax.axis_size("date")

    def heads(a):
        return a.reshape(pixels, dates, 8, 128).transpose(0, 2, 1, 3)

    any_ = pl.BlockSpec(memory_space=pl.ANY)
    vm = pl.BlockSpec(memory_space=pltpu.VMEM)
    four = (8, NT, 4, 128)

    def v(shape, dtype):
        return pltpu.VMEM(shape, dtype)

    sm = pltpu.SMEM
    scratch = [
        sm((4,), jnp.int32), v((4, NT), jnp.int32), v((2, 1024), F32), v((264, 1024), BF16), sm((8,), F32), sm((8,), F32), sm((8,), F32),
        v(four, BF16), v((LEN, 1024), BF16), v((128, 1024), BF16), v((LEN, 128), F32), v((3, NT, 4, 128), BF16),
        v((3, NT, 4, 128), BF16), v(four, BF16), v(four, BF16), v((LEN, 128), F32), v((8, LEN), F32), v((8, LEN), F32),
        v((LEN, LEN), F32), v((LEN, LEN), F32), v((8, LEN), F32), v((8, LEN), F32), v((8, 128), F32), v((128, LEN), F32),
        v(four, BF16), v((3, NT, 4, 128), BF16),
        v((3, NT, 4, 128), BF16), v((8, 128, 128), F32), v((8, 128, 128), BF16), v((8, 128, 128), BF16),
        v((8, 128, 128), BF16), v((8, 128, 128), BF16), v((128, 128), F32), v((8, 16, 128), BF16), v((8, 16, 128), BF16),
        v((16, 128), F32), v((8, 16, 128), F32), v((8, 16, 128), BF16), v((8, 8, 16, 128), BF16), v((8, 8, 16, 128), BF16),
        v((9, 8, 128), F32), v((9, 8, 128), F32), v((8, 2, 8, 128), F32), v((8, 2, 8, 128), F32), v((2, 8, 128), F32),
        v((8, 2, 8, 128), F32), v((2, 8, 128), F32), v((8, 2, 8, 128), F32), v((8, 128), F32), v((8, 8, 128), F32),
        pltpu.SemaphoreType.DMA((7,)), pltpu.SemaphoreType.DMA((8,)), pltpu.SemaphoreType.DMA((5,)), pltpu.SemaphoreType.DMA((18,)),
        pltpu.SemaphoreType.DMA((18,)), pltpu.SemaphoreType.DMA((8,)), pltpu.SemaphoreType.DMA((8,)),
    ]

    def kernel(*refs):
        body(1.0 / math.sqrt(total), *refs)

    vg, ig, wg, tg, hg = pl.pallas_call(
        kernel,
        name="mixer_backward",
        out_shape=(
            v((pixels, 8, dates, 128), BF16), v(four, BF16), v((264, 1024), F32),
            v((2, 1024), F32), v((3, 8), F32),
        ),
        in_specs=[any_] * 10,
        out_specs=(vm, vm, vm, vm, vm),
        scratch_shapes=scratch,
        compiler_params=pltpu.CompilerParams(collective_id=0, has_side_effects=True),
    )(
        heads(layer_input), heads(head_input), heads(out_grad), sensor_ids, valid_mask.T, sensor_table, proj_weight.T,
        step_bias, decay_log, skip_gain,
    )

    six = jax.ShapeDtypeStruct((pixels, 8, dates, 128), BF16)
    vg, ig, wg, tg, hg = pl.pallas_call(
        write_out,
        name="write_outputs",
        out_shape=(six, six, *(jax.ShapeDtypeStruct(a.shape, a.dtype) for a in (wg, tg, hg))),
        in_specs=[vm] * 5,
        out_specs=(any_,) * 5,
        scratch_shapes=[pltpu.SemaphoreType.DMA((17,))],
    )(*(pltpu.with_memory_space_constraint(a, pltpu.VMEM) for a in (vg, ig, wg, tg, hg)))

    def dates_first(a):
        return a.transpose(0, 2, 1, 3).reshape(pixels, dates, width)

    return dates_first(vg), dates_first(ig), wg.T, tg, hg


def solution(mesh):
    in_specs = (
        P("tile", "date", None), P("tile", "date", None), P("tile", "date", None), P("date"), P("tile", "date"),
        P(), P(), P(), P(), P(),
    )
    out_specs = (P("tile", "date", None), P("tile", "date", None), P(), P(), P())
    return jax.shard_map(on_device, mesh=mesh, in_specs=in_specs, out_specs=out_specs, check_vma=False)
```
